32 devices in a mesh: tier: 16 (over z, x, core), sys: 2 (over y).
Axes of the slice: x: 2, y: 2, z: 4, core: 2. Of those that a mesh axis runs over, the one named last changes fastest.
Arguments:
- state: float32 [64, 2, 512, 512], P('tier', None, 'sys'), may hold values from -6 to 6
- slope: float32 [64, 2, 512, 512], P('tier', None, 'sys'), may hold values from -6 to 6
- counts: int32 [16], replicated, may hold values from 1 to 4, 32 in all
- links: int32 [4, 64, 24], P(None, 'tier'), may hold values from 0 to 63, as said below
- mode_site: int32 [12], replicated, may hold values from 0 to 511, as said below
- mode_coef: float32 [2, 12], replicated, may hold values from -3 to 3
- mode_rate: float32 [12], replicated, may hold values from 0.01 to 0.1
- h_bands: float32 [9, 512], replicated, may hold values from -3 to 3
Outputs:
- slope_next: float32 [64, 2, 512, 512], P('tier', None, 'sys')
- partial_sum: float32 [64, 2, 512, 512], P('tier', None, 'sys')
The draws below stay inside these ranges and needn't reach their ends.
Inputs may be any that keep to these rules, and one draw needn't show every extreme that they name: Index d of tier holds counts[d] live auxiliary operators, in its first slots; the counts sum to 32. links[0] is a global slot (index of tier times 4 plus the slot), links[1] a mode below 12, links[2] is 0 or 1, links[3] is 1 or 2. Each slot has exactly one link with direction 0 and one with direction 1 for every mode. Of the 96 links of the slots of one index of tier, exactly 6 name slots of each index of tier; of the links whose mode k has k // 6 equal to one row block's number, at most 4 name slots of one index of tier, and in every row block some index of tier is named by exactly 4 of them. `mode_site`: mode k's site lies in row block k // 6, that is in rows (k // 6) * 256 to (k // 6) * 256 + 255; the sites are distinct.
All inputs are finite; a program needn't handle non-finite values.
Results may differ from the reference program's by a relative error of at most 0.0003.
Values sent between devices are 32-bit elements; how exact they have to be, the bound alone decides.
A program may use at most 64 MiB of HBM per device.

```python
import math
import jax
import jax.numpy as jnp
import numpy as np
from jax import lax

LEVELS = 512
BAND = 8
MODES_BLK = 6
SLOTS = 4
SLOTS_ALL = 64
ADOS = 32
MODES = 12
LINKS = 24
ROWS_DEV = 256
N_TIER = 16
N_SYS = 2


def draw_links(key, part):
    per_block = SLOTS * 2 * MODES_BLK

    def one_device(device_key):
        key_holder, key_order, key_slot, key_level = jax.random.split(device_key, 4)
        holders = jax.random.permutation(key_holder, N_TIER).astype(jnp.int32)
        order = jax.vmap(lambda block_key: jax.random.permutation(block_key, per_block))(jax.random.split(key_order, N_SYS)).astype(jnp.int32)
        base = jnp.arange(N_SYS, dtype=jnp.int32)[:, None] * per_block + order
        holder = holders[base // 2 % N_TIER]
        within = jnp.arange(per_block, dtype=jnp.int32)
        target_slot = jax.random.randint(key_slot, (N_SYS, per_block), 0, SLOTS, dtype=jnp.int32)
        mode_pick = jnp.arange(N_SYS, dtype=jnp.int32)[:, None] * MODES_BLK + (within // 2 % MODES_BLK)[None, :]
        link_kind = jnp.broadcast_to((within % 2)[None, :], (N_SYS, per_block))
        link_level = jax.random.randint(key_level, (N_SYS, per_block), 1, 3, dtype=jnp.int32)
        stacked = jnp.stack([holder * SLOTS + target_slot, mode_pick, link_kind, link_level])
        stacked = stacked.reshape(4, N_SYS, SLOTS, 2 * MODES_BLK)
        return jnp.transpose(stacked, (0, 2, 1, 3)).reshape(4, SLOTS, LINKS)
    devices = jax.vmap(one_device)(jax.random.split(jax.random.fold_in(key, 11), N_TIER))
    return jnp.transpose(devices, (1, 0, 2, 3)).reshape(4, SLOTS_ALL, LINKS).astype(jnp.int32)


def draw_mode_site(key, part):

    def one_block(block_key):
        return jax.random.permutation(block_key, ROWS_DEV)[:MODES_BLK].astype(jnp.int32)
    chosen = jax.vmap(one_block)(jax.random.split(jax.random.fold_in(key, 23), N_SYS))
    offsets = ROWS_DEV * jnp.arange(N_SYS, dtype=jnp.int32)[:, None]
    return (chosen + offsets).reshape(MODES).astype(jnp.int32)


def level_of(own_key, shape, shards, least, top_value):
    def one(axis_at, parts):
        steps = jax.random.uniform(jax.random.fold_in(jax.random.fold_in(own_key, 6), axis_at), (parts,), jnp.float32, least / len(shards), top_value / len(shards))
        return jnp.repeat(jnp.exp(steps), shape[axis_at] // parts).reshape((-1,) + (1,) * (len(shape) - axis_at - 1))

    level = one(*shards[0])
    for cut in shards[1:]:
        level = level * one(*cut)
    return level


def length_profile(count, total, bound, lean):
    loads = [(1 << 20) // math.isqrt(grade ** lean) + 1 for grade in range(2, count + 1)]
    spare, given = total - bound - (count - 1), [1] * (count - 1)
    while spare > 0:
        movable = [i for i in range(count - 1) if given[i] < bound]
        whole, remaining = sum([loads[i] for i in movable]), spare
        for i in movable:
            more = min(bound - given[i], max(1, remaining * loads[i] // whole), spare)
            given[i] = given[i] + more
            spare = spare - more
    return np.array([bound] + given)


def ragged_sizes(stream_key, count, total, reach, lean):
    if count == 2:
        one = jax.random.randint(stream_key, (), max(1, total - reach), min(reach, total - 1) + 1)
        return jnp.stack([one, total - one])
    lengths = jnp.asarray(length_profile(count, total, reach, lean), jnp.int32)
    twos = (count - 1) // 2
    source_of, sink = lengths[1:1 + 2 * twos:2], lengths[2:2 + 2 * twos:2]
    slack = jnp.minimum(source_of - 1, reach - sink)
    shifted = jax.random.randint(jax.random.fold_in(stream_key, 1), (twos,), 0, 1 << 20) % (slack + 1)
    lengths = lengths.at[1:1 + 2 * twos:2].set(source_of - shifted).at[2:2 + 2 * twos:2].set(sink + shifted)
    return lengths[jax.random.permutation(jax.random.fold_in(stream_key, 2), count)]


def centred(rng, extent, width, most, shards=(), kind=jnp.bfloat16):
    values = width * jax.random.normal(rng, extent, jnp.float32)
    if shards:
        values = values * level_of(rng, extent, shards, -0.22, 0.18)
    return jnp.clip(values, -most, most).astype(kind)


def setup_inputs(seed: int = 0) -> dict:
    seeds = jax.random.split(jax.random.key(seed), 9)
    state = centred(seeds[0], (SLOTS_ALL, 2, LEVELS, LEVELS), 1.0, 6.0, ((0, 16), (2, 2)), jnp.float32)
    slope = centred(seeds[1], (SLOTS_ALL, 2, LEVELS, LEVELS), 1.0, 6.0, ((0, 16), (2, 2)), jnp.float32)
    counts = ragged_sizes(seeds[2], N_TIER, ADOS, SLOTS, 2).astype(jnp.int32)
    links = draw_links(jax.random.fold_in(seeds[8], 71), 0)
    mode_site = draw_mode_site(jax.random.fold_in(seeds[8], 71), 0)
    mode_coef = centred(seeds[5], (2, MODES), 0.5, 3.0, (), jnp.float32)
    mode_rate = jnp.clip(jnp.exp(jax.random.uniform(seeds[6], (MODES,), jnp.float32, math.log(0.01), math.log(0.1))), 0.01, 0.1)
    h_bands = centred(seeds[7], (BAND + 1, LEVELS), 0.5, 3.0, (), jnp.float32)
    return {"state": state, "slope": slope, "counts": counts, "links": links, "mode_site": mode_site, "mode_coef": mode_coef, "mode_rate": mode_rate, "h_bands": h_bands}


step_size = 0.05


def shifted_band(h_bands):
    band_width = h_bands.shape[0] - 1
    length = h_bands.shape[1]
    padded = jnp.pad(h_bands, ((0, 0), (band_width, 0)))
    return jnp.stack([padded[offset, band_width - offset:band_width - offset + length] for offset in range(band_width + 1)])


def band_rows(padded, upper_band, lower_band, band_width):
    length = upper_band.shape[1]
    summed = upper_band[0][:, None] * padded[..., band_width:band_width + length, :]
    for offset in range(1, band_width + 1):
        summed = summed + upper_band[offset][:, None] * padded[..., band_width + offset:band_width + offset + length, :]
        summed = summed + lower_band[offset][:, None] * padded[..., band_width - offset:band_width - offset + length, :]
    return summed


def band_cols(field, upper_band, lower_band, band_width):
    length = field.shape[-1]
    padded = jnp.pad(field, ((0, 0),) * (field.ndim - 1) + ((band_width, band_width),))
    summed = upper_band[0] * field
    for offset in range(1, band_width + 1):
        summed = summed + upper_band[offset] * padded[..., band_width + offset:band_width + offset + length]
        summed = summed + lower_band[offset] * padded[..., band_width - offset:band_width - offset + length]
    return summed


def reference(state, slope, counts, links, mode_site, mode_coef, mode_rate, h_bands):
    midpoint = state + (0.5 * step_size) * slope
    every_slot = jnp.arange(SLOTS_ALL, dtype=jnp.int32)
    live = (every_slot % SLOTS < counts[every_slot // SLOTS]).astype(jnp.float32)
    lower_band = shifted_band(h_bands)

    def derive(carry, inputs):
        field, link_set = inputs
        neighbour = link_set[0]
        link_mode = link_set[1]
        link_kind = link_set[2]
        link_level = link_set[3].astype(jnp.float32)
        sites = mode_site[link_mode]
        downward = link_kind == 1
        neighbour_live = live[neighbour]
        weight_re = jnp.where(downward, link_level * mode_coef[0][link_mode], 1.0) * neighbour_live
        weight_im = jnp.where(downward, link_level * mode_coef[1][link_mode], 0.0) * neighbour_live
        damping = jnp.sum(jnp.where(downward, link_level * mode_rate[link_mode], 0.0))
        column_part = midpoint[neighbour, :, :, sites]
        row_part = midpoint[neighbour, :, sites, :]
        padded = jnp.pad(field, ((0, 0), (BAND, BAND), (0, 0)))
        commuted = band_rows(padded, h_bands, lower_band, BAND) - band_cols(field, h_bands, lower_band, BAND)
        deriv_re = commuted[1] - damping * field[0]
        deriv_im = -commuted[0] - damping * field[1]
        col_re = -(weight_re[:, None] * column_part[:, 1] - weight_im[:, None] * column_part[:, 0])
        col_im = weight_re[:, None] * column_part[:, 0] + weight_im[:, None] * column_part[:, 1]
        row_re = weight_re[:, None] * row_part[:, 1] + weight_im[:, None] * row_part[:, 0]
        row_im = -(weight_re[:, None] * row_part[:, 0] - weight_im[:, None] * row_part[:, 1])
        deriv_re = deriv_re.at[:, sites].add(col_re.T)
        deriv_im = deriv_im.at[:, sites].add(col_im.T)
        deriv_re = deriv_re.at[sites, :].add(row_re)
        deriv_im = deriv_im.at[sites, :].add(row_im)
        return carry, jnp.stack([deriv_re, deriv_im])

    _, derived = lax.scan(derive, jnp.zeros((), jnp.float32), (midpoint, jnp.moveaxis(links, 1, 0)))
    slope_next = derived * live[:, None, None, None]
    partial_sum = (state + (step_size / 6.0) * slope + (step_size / 3.0) * slope_next) * live[:, None, None, None]
    return slope_next, partial_sum
```

```python
import functools

import jax
import jax.numpy as jnp
from jax import lax
from jax.experimental import pallas as pl
from jax.experimental.pallas import tpu as pltpu
from jax.sharding import PartitionSpec as P

step_size = 0.05
MESH = pl.DeviceIdType.MESH
f32 = jnp.float32
bf16 = jnp.bfloat16


def up(value, unit):
    return (value + unit - 1) // unit * unit


def split(value):
    hi = value.astype(bf16)
    lo = (value - hi.astype(f32)).astype(bf16)
    return hi, lo


def mm(a, b):
    return lax.dot_general(a, b, (((1,), (0,)), ((), ())), preferred_element_type=f32)


def mm_nt(a, b):
    return lax.dot_general(a, b, (((1,), (1,)), ((), ())), preferred_element_type=f32)


def mm3(a, b):
    a_hi, a_lo = split(a)
    b_hi, b_lo = split(b)
    return mm(a_hi, b_hi) + (mm(a_hi, b_lo) + mm(a_lo, b_hi))


def exchange_kernel(
    dims,
    links_hbm,
    counts_hbm,
    site_hbm,
    coef_hbm,
    rate_hbm,
    bands_hbm,
    state_hbm,
    slope_hbm,
    d_buf,
    base_ref,
    c_ref,
    r_ref,
    spread_ref,
    row_at_ref,
    links_ref,
    counts_ref,
    site_ref,
    coef_ref,
    rate_ref,
    bands_ref,
    st,
    sl,
    z_hi,
    z_lo,
    h_hi,
    h_lo,
    req_ref,
    req_in,
    halo_out,
    halo_in,
    cross_hi,
    cross_lo,
    col_hi,
    col_lo,
    row_pack,
    send_buf,
    recv_buf,
    load_sem,
    req_send,
    req_recv,
    halo_send,
    halo_recv,
    pack_send,
    pack_recv,
    small_sem,
    here_sem,
    near_sem,
):
    tiers, systems, group, slots, modes, block, edge, per_slot, rp, cj, rw = dims
    rows, levels = st[0].shape
    me = lax.axis_index("tier")
    sy = lax.axis_index("sys")
    planes = slots * 2
    layers = tiers // group
    layer = me // group
    wide_m = spread_ref.shape[0]
    parts = 2 * rows // 128
    per_tile = 8 // parts
    tiles = cj // per_tile
    visits = order(layers, layer)
    place_in = me - layer * group
    first = layer * group

    def load(p):
        g, c = p // 2, p % 2
        return (
            pltpu.make_async_copy(state_hbm.at[g, c], st[p], load_sem.at[0, p]),
            pltpu.make_async_copy(slope_hbm.at[g, c], sl[p], load_sem.at[1, p]),
        )

    small = [
        pltpu.make_async_copy(src, dst, small_sem.at[n])
        for n, (src, dst) in enumerate(
            (
                (links_hbm, links_ref),
                (counts_hbm, counts_ref),
                (site_hbm, site_ref),
                (coef_hbm, coef_ref),
                (rate_hbm, rate_ref),
                (bands_hbm, bands_ref),
            )
        )
    ]
    for copy in small:
        copy.start()

    barrier = pltpu.get_barrier_semaphore()

    turns = [lax.rem(place_in + i, group) for i in range(group)]

    def greet(t):
        pl.semaphore_signal(barrier, inc=1, device_id=(t, sy), device_id_type=MESH)

    def mates(act):
        for i in range(1, group):
            act(first + turns[i])

    def layer_at(step, act):
        @pl.when((layer + step >= 0) & (layer + step < layers))
        def _():
            for i in range(group):
                act((layer + step) * group + turns[i])

    mates(greet)
    for step in range(1, layers):
        layer_at(step, greet)

    @pl.when(sy < systems - 1)
    def _():
        pl.semaphore_signal(barrier, inc=1, device_id=(me, sy + 1), device_id_type=MESH)

    for p in range(planes):
        for copy in load(p):
            copy.start()

    total = slots * per_slot
    wide_q = up(total, 128)

    def iota(shape, axis):
        return lax.broadcasted_iota(jnp.int32, shape, axis).astype(f32)

    def flag(where):
        return jnp.where(where, 1.0, 0.0)

    for copy in small:
        copy.wait()
    flat = jnp.zeros((4, wide_q), f32)
    for g in range(slots):
        place = flag(
            iota((per_slot, wide_q), 1) == iota((per_slot, wide_q), 0) + float(g * per_slot)
        )
        flat += mm(links_ref[:, g, :].astype(f32).astype(bf16), place.astype(bf16))
    lane_q = iota((1, wide_q), 1)
    valid = lane_q < float(total)
    mode, kind, level = flat[1:2], flat[2:3], flat[3:4]
    holder = jnp.floor((flat[0:1] + 0.5) * (1.0 / slots))
    target = flat[0:1] - holder * float(slots)
    holder = jnp.where(valid, holder, -1.0)
    slot_of = jnp.where(valid, jnp.floor((lane_q + 0.5) * (1.0 / per_slot)), -1.0)
    first_mode = (sy * block).astype(f32)
    in_block = valid & (mode >= first_mode) & (mode < first_mode + float(block))
    local_mode = mode - first_mode
    has = flag(holder == iota((tiers, wide_q), 0))
    has_r = has * flag(in_block)
    before = flag(iota((wide_q, wide_q), 0) < iota((wide_q, wide_q), 1)).astype(bf16)
    rank_c = jnp.sum(has * mm(has.astype(bf16), before), axis=0, keepdims=True)
    rank_r = jnp.sum(has_r * mm(has_r.astype(bf16), before), axis=0, keepdims=True)
    lane_j = iota((128, wide_q), 0)

    def asked(codes, ranks):
        return mm_nt(codes.astype(bf16), flag(lane_j == ranks).astype(bf16))

    req = asked(has * (target * float(wide_m) + mode + 1.0), rank_c) - 1.0
    for c in range(2):
        code = (target + float(c * slots)) * float(block) + local_mode + 1.0
        req += asked(has_r * code, rank_r + float(8 + c * rp))
    for t in range(tiers):
        req_ref[t] = req[t : t + 1, :]
    req_in[me] = req_ref[me]

    def request(t, other):
        return pltpu.make_async_remote_copy(
            src_ref=req_ref.at[t],
            dst_ref=req_in.at[other],
            send_sem=req_send.at[t],
            recv_sem=req_recv.at[other],
            device_id=(t, sy),
            device_id_type=MESH,
        )

    def ask(t):
        request(t, me).start()

    def announce(t):
        pl.semaphore_signal(here_sem.at[layer], inc=1, device_id=(t, sy), device_id_type=MESH)

    pl.semaphore_wait(barrier, first + group - 1 + (sy > 0).astype(jnp.int32))
    for step in range(layers - 1, 0, -1):
        layer_at(-step, announce)

    @pl.when(sy > 0)
    def _():
        pl.semaphore_signal(near_sem, inc=1, device_id=(me, sy - 1), device_id_type=MESH)

    for step in range(layers - 1, 0, -1):
        layer_at(-step, ask)
    mates(ask)

    def ask_above(step):
        @pl.when(layer + step < layers)
        def _():
            pl.semaphore_wait(here_sem.at[layer + step], group)

        layer_at(step, ask)

    row_pack[...] = jnp.zeros_like(row_pack)
    col_hi[...] = jnp.zeros_like(col_hi)
    col_lo[...] = jnp.zeros_like(col_lo)
    site_lane = lax.broadcasted_iota(jnp.int32, (1, levels), 1)
    spread_ref[...] = jnp.zeros_like(spread_ref)
    for k in range(modes):
        spread_ref[k : k + 1, :] = flag(site_lane == site_ref[k])
    pick = spread_ref[...].astype(bf16)
    for g in range(slots):
        for c in range(2):
            p = g * 2 + c
            for copy in load(p):
                copy.wait()
            mid = st[p][...] + (0.5 * step_size) * sl[p][...]
            halo_out[0, p] = mid[rows - edge :, :]
            halo_out[1, p] = mid[:edge, :]
            hi, lo = split(mid)
            z_hi[p] = hi
            z_lo[p] = lo
            at = slice(g * wide_m, (g + 1) * wide_m)
            for dest, part in ((col_hi, hi), (col_lo, lo)):
                cols = mm_nt(pick, part).astype(bf16)
                for h in range(-(-rows // 128)):
                    q = c * rows // 128 + h
                    lane = c * rows % 128
                    dest[q, at, lane : lane + min(rows, 128)] = cols[:, h * 128 : h * 128 + 128]
            for k in range(block):
                at = jnp.clip(site_ref[sy * block + k] - sy * rows, 0, rows - 1)
                row = st[p][pl.ds(at, 1), :] + (0.5 * step_size) * sl[p][pl.ds(at, 1), :]
                dest = (c * slots + g) * block + k
                row_pack[dest : dest + 1, :] = row
            for step in range(1, layers):
                if p == planes * step // (layers - 1) - 1:
                    ask_above(step)

    def halo(side):
        return pltpu.make_async_remote_copy(
            src_ref=halo_out.at[side],
            dst_ref=halo_in.at[side],
            send_sem=halo_send.at[side],
            recv_sem=halo_recv.at[side],
            device_id=(me, sy + 1 if side == 0 else sy - 1),
            device_id_type=MESH,
        )

    @pl.when(sy > 0)
    def _():
        halo(1).start()

    @pl.when(sy < systems - 1)
    def _():
        pl.semaphore_wait(near_sem, 1)
        halo(0).start()

    @pl.when(sy == 0)
    def _():
        halo_in[0] = jnp.zeros_like(halo_in[0])

    @pl.when(sy == systems - 1)
    def _():
        halo_in[1] = jnp.zeros_like(halo_in[1])

    def pack(n, turn, t, other):
        at = pl.multiple_of((n * group + turn) * rw, rw)
        return pltpu.make_async_remote_copy(
            src_ref=send_buf.at[pl.ds(at, rw), :],
            dst_ref=recv_buf.at[pl.ds(pl.multiple_of(other * rw, rw), rw), :],
            send_sem=pack_send.at[n * group + turn],
            recv_sem=pack_recv.at[other],
            device_id=(t, sy),
            device_id_type=MESH,
        )

    def calls(act):
        for n in range(layers):
            for i in range(1 if n == layers - 1 else 0, group):
                act(n, turns[i], visits[n] * group + turns[i])

    row_hi, row_lo = split(row_pack[...])
    per_c, per_r = tiles * group * 8, group * rw
    index = iota((per_c, 128), 0)
    tile = jnp.floor((index + 0.5) * (1.0 / (group * 8)))
    index -= tile * float(group * 8)
    owner = jnp.floor((index + 0.5) * (1.0 / 8))
    index -= owner * 8.0
    column = jnp.floor((index + 0.5) * (1.0 / parts))
    part_of = index - column * float(parts)
    wanted = tile * float(per_tile) + column
    index = iota((per_r, 128), 0)
    owner_r = jnp.floor((index + 0.5) * (1.0 / rw))
    wanted_r = index - owner_r * float(rw) + 8.0
    owner = jnp.concatenate([owner, owner_r], axis=0)
    spot = flag(jnp.concatenate([wanted, wanted_r], axis=0) == iota((per_c + per_r, 128), 1))
    expand = flag(owner[:, 0:1] == iota((per_c + per_r, group), 1)).astype(bf16)
    wide_k = parts * slots * wide_m
    wanted_at = iota((per_c, wide_k), 1) - part_of[:, 0:1] * float(slots * wide_m)
    in_part = (wanted_at >= 0.0) & (wanted_at < float(slots * wide_m))
    wanted_at = jnp.where(in_part, wanted_at, -2.0)
    wanted_row = iota((per_r, row_pack.shape[0]), 1)
    for n in range(layers):
        start = visits[n] * group
        for i in range(1 if n == layers - 1 else 0, group):
            request(start + turns[i], start + turns[i]).wait_recv()
        codes = mm(expand, req_in[pl.ds(start, group), 0, :].astype(bf16))
        code = jnp.sum(codes * spot, axis=1, keepdims=True)
        pick_c = flag(code[:per_c] == wanted_at).astype(bf16)
        pick_r = flag(code[per_c:] == wanted_row).astype(bf16)
        packed = mm(pick_c, col_hi[...].reshape(wide_k, 128)) + mm(
            pick_c, col_lo[...].reshape(wide_k, 128)
        )
        here = slice(n * group * rw, (n + 1) * group * rw)
        send_buf[here, 0:levels] = mm(pick_r, row_hi) + mm(pick_r, row_lo)
        for k in range(tiles):
            send_buf[here, levels + k * 128 : levels + (k + 1) * 128] = packed[
                k * group * 8 : (k + 1) * group * 8
            ]
        for i in range(1 if n == layers - 1 else 0, group):
            pack(n, turns[i], start + turns[i], me).start()
    own = pl.multiple_of(((layers - 1) * group + place_in) * rw, rw)
    recv_buf[pl.ds(pl.multiple_of(me * rw, rw), rw), :] = send_buf[pl.ds(own, rw), :]

    row_start = sy * rows
    blocks = levels // 128
    over = h_hi.shape[1] // 128
    diff = lax.broadcasted_iota(jnp.int32, (128, 128), 0) - lax.broadcasted_iota(
        jnp.int32, (128, 128), 1
    )
    bands = bands_ref[...]
    moved = [bands[o : o + 1, :] if o == 0 else pltpu.roll(bands, o, 1)[o : o + 1, :] for o in range(edge + 1)]

    def block_of(row, b):
        return row[:, b * 128 : (b + 1) * 128]

    def keep(hi_ref, lo_ref, n, row, lane, value):
        hi, lo = split(-value)
        high, wide = value.shape
        hi_ref[n, row : row + high, lane : lane + wide] = hi
        lo_ref[n, row : row + high, lane : lane + wide] = lo

    for ref in (h_hi, h_lo, cross_hi, cross_lo):
        ref[...] = jnp.zeros_like(ref)
    for b in range(blocks):
        value = jnp.where(diff == 0, block_of(bands[0:1, :], b), 0.0)
        for o in range(1, edge + 1):
            value = jnp.where(diff == o, block_of(bands[o : o + 1, :], b), value)
            value = jnp.where(diff == -o, block_of(moved[o], b), value)
        n, at = b // over, b % over * 128
        keep(h_hi, h_lo, n, at, at, value)
    corner = 2 * edge
    slant = diff[0:corner, :]
    for b in range(blocks - 1):
        above = jnp.zeros((corner, 128), f32)
        below = jnp.zeros((corner, 128), f32)
        for o in range(1, edge + 1):
            above = jnp.where(slant == corner - o, block_of(moved[o], b + 1), above)
            below = jnp.where(slant == o - 128, block_of(bands[o : o + 1, :], b), below)
        n, at = b // over, b % over * 128
        if b % over < over - 1:
            keep(h_hi, h_lo, n, at + 128 - corner, at + 128, above)
            keep(h_hi, h_lo, n, at + 128, at, below)
        else:
            keep(cross_hi, cross_lo, 2 * n, 0, at, below)
            keep(cross_hi, cross_lo, 2 * n + 1, 128 - corner, 0, above)

    def rolled(shift):
        return pltpu.roll(bands, lax.rem(shift + 2 * levels, levels), 1)

    if rows == h_hi.shape[1]:
        loc_hi, loc_lo = -h_hi[sy], -h_lo[sy]
    else:
        wide_r = up(rows, 128)
        gap = lax.broadcasted_iota(jnp.int32, (rows, wide_r), 0) - lax.broadcasted_iota(
            jnp.int32, (rows, wide_r), 1
        )
        near_bands = rolled(-row_start)
        loc = jnp.where(gap == 0, near_bands[0:1, :wide_r], 0.0)
        for o in range(1, edge + 1):
            loc = jnp.where(gap == o, near_bands[o : o + 1, :wide_r], loc)
            loc = jnp.where(gap == -o, pltpu.roll(near_bands, o, 1)[o : o + 1, :wide_r], loc)
        loc_hi, loc_lo = split(loc[:, :rows])
    sub = lax.broadcasted_iota(jnp.int32, (2 * edge, 128), 0)
    lan = lax.broadcasted_iota(jnp.int32, (2 * edge, 128), 1)
    low_bands = rolled(edge - row_start)
    high_bands = rolled(edge - row_start - rows)
    halo_h = jnp.zeros((2 * edge, 128), f32)
    for o in range(edge + 1):
        low = (sub < edge) & (lan < edge) & (edge + sub - lan == o)
        high = (sub >= edge) & (lan >= edge) & (lan < 2 * edge) & (edge + lan - sub == o)
        above = pltpu.roll(high_bands, o, 1) if o else high_bands
        halo_h = jnp.where(low, low_bands[o : o + 1, :128], halo_h)
        halo_h = jnp.where(high, above[o : o + 1, :128], halo_h)
    ghost_hi, ghost_lo = split(halo_h)
    ghost_h = jnp.where(lan < 2 * edge, ghost_hi.astype(f32), 0.0)
    ghost_h += pltpu.roll(jnp.where(lan < 2 * edge, ghost_lo.astype(f32), 0.0), 2 * edge, 1)
    ghost_h += pltpu.roll(jnp.where(lan < 2 * edge, ghost_hi.astype(f32), 0.0), 4 * edge, 1)
    ghost_h = ghost_h.astype(bf16)

    def table(ref, count, index):
        value = jnp.zeros((1, wide_q), f32)
        for k in range(count):
            value = jnp.where(index == float(k), ref(k), value)
        return value

    own_count = counts_ref[me].astype(f32)
    near = flag(target < table(lambda k: counts_ref[k].astype(f32), tiers, holder))
    near = near * flag(slot_of < own_count)
    down = kind == 1.0
    w_re = jnp.where(down, level * table(lambda k: coef_ref[0, k], modes, mode), 1.0) * near
    w_im = jnp.where(down, level * table(lambda k: coef_ref[1, k], modes, mode), 0.0) * near
    rate = jnp.where(down, level * table(lambda k: rate_ref[k], modes, mode), 0.0)
    wide_b = row_at_ref.shape[0]

    def mixing(wide, index, mask, signs):
        from_re, from_im = [], []
        for g in range(slots):
            own = flag((iota((wide, wide_q), 0) == index) & (slot_of == float(g)) & mask)
            for re, im in signs:
                from_re.append(own * re)
                from_im.append(own * im)
        return jnp.concatenate(from_re, axis=0), jnp.concatenate(from_im, axis=0)

    def packets(count, at, mask):
        return flag((iota((count, wide_q), 0) == at) & mask).astype(bf16)

    def place(value, at):
        hi, lo = split(value)
        return mm_nt(hi, at) + mm_nt(lo, at)

    rank_tile = jnp.floor((rank_c + 0.5) * (1.0 / per_tile))
    at_tile = rank_tile * float(tiers * 8) + holder * 8.0
    at_tile += (rank_c - rank_tile * float(per_tile)) * float(parts)
    from_re, from_im = mixing(wide_m, mode, valid, ((w_im, -w_re), (w_re, w_im)))

    def column_mix(value, q):
        return place(value, packets(tiles * tiers * 8, at_tile + float(q), valid))

    if rows < 128:
        mix_c = [column_mix(from_re, 0), column_mix(from_im, 0)]
    else:
        mix_c = [
            column_mix(from_re, h) + column_mix(from_im, parts // 2 + h) for h in range(parts // 2)
        ]
    from_re, from_im = mixing(wide_b, local_mode, in_block, ((w_im, w_re), (-w_re, w_im)))
    at_row = holder * float(rw) + rank_r
    mix_r = place(from_re, packets(tiers * rw, at_row, in_block)) + place(
        from_im, packets(tiers * rw, at_row + float(rp), in_block)
    )
    row_lane = lax.broadcasted_iota(jnp.int32, (1, rows), 1)
    row_at_ref[...] = jnp.zeros_like(row_at_ref)
    for k in range(block):
        row_at_ref[k : k + 1, :] = flag(row_lane == site_ref[sy * block + k] - row_start)

    def dots(pairs):
        if rows % 128 == 0:
            return mm(
                jnp.concatenate([a for a, _ in pairs], axis=1),
                jnp.concatenate([b for _, b in pairs], axis=0),
            )
        return sum(mm(a, b) for a, b in pairs)

    width = h_hi.shape[1]
    cuts = levels // width

    def commute(p, n):
        hi, lo = z_hi.at[p], z_lo.at[p]
        at = slice(n * width, (n + 1) * width)
        near_hi, near_lo = hi[:, at], lo[:, at]
        pairs = [(loc_hi, near_hi), (loc_lo, near_hi), (loc_hi, near_lo)]
        pairs += [(near_hi, h_hi[n]), (near_hi, h_lo[n]), (near_lo, h_hi[n])]
        for side, there in ((2 * n, (n + 1) * width), (2 * n - 1, n * width - 128)):
            if 0 <= side < 2 * (cuts - 1):
                there = slice(there, there + 128)
                pairs += [(hi[:, there], cross_hi[side]), (hi[:, there], cross_lo[side])]
                pairs += [(lo[:, there], cross_hi[side])]
        return dots(pairs)

    def ghost(p):
        hi, lo = split(jnp.concatenate([halo_in[s, p] for s in range(2)], axis=0))
        rest = jnp.zeros((128 - 6 * edge, levels), bf16)
        return mm(ghost_h, jnp.concatenate([hi, hi, lo, rest], axis=0))

    for g in range(slots):
        live = flag(own_count > float(g))
        damp = jnp.sum(jnp.where(slot_of == float(g), rate, 0.0), axis=1, keepdims=True) * live
        for c in range(2):
            p = g * 2 + c
            sign = live if c == 0 else -live
            for n in range(cuts):
                at = slice(n * width, (n + 1) * width)
                mid = st[p][:, at] + (0.5 * step_size) * sl[p][:, at]
                d_buf[p, :, at] = sign * commute(g * 2 + 1 - c, n) - damp * mid
                base_ref[p, :, at] = live * (st[p][:, at] + (step_size / 6.0) * sl[p][:, at])

    @pl.when(sy > 0)
    def _():
        halo(0).wait_recv()

    @pl.when(sy < systems - 1)
    def _():
        halo(1).wait_recv()

    for g in range(slots):
        live = flag(own_count > float(g))
        for c in range(2):
            extra = (live if c == 0 else -live) * ghost(g * 2 + 1 - c)
            d_buf[g * 2 + c, 0:edge, :] += extra[0:edge]
            d_buf[g * 2 + c, rows - edge : rows, :] += extra[edge : 2 * edge]

    calls(lambda n, turn, t: pack(n, turn, t, t).wait_recv())
    got_c = jnp.concatenate(
        [recv_buf[:, levels + n * 128 : levels + (n + 1) * 128] for n in range(tiles)], axis=0
    )
    got_r = recv_buf[:, 0:levels]
    r_ref[...] = mm3(mix_r, got_r)
    if rows < 128:
        c_ref[...] = mm3(mix_c[0], got_c[:, :rows]) + mm3(mix_c[1], got_c[:, rows:])
    else:
        for h in range(parts // 2):
            c_ref[:, h * 128 : (h + 1) * 128] = mm3(mix_c[h], got_c)

    calls(lambda n, turn, t: request(t, me).wait_send())
    calls(lambda n, turn, t: pack(n, turn, t, me).wait_send())

    @pl.when(sy < systems - 1)
    def _():
        halo(0).wait_send()

    @pl.when(sy > 0)
    def _():
        halo(1).wait_send()


def finish_kernel(
    cuts, spread_ref, row_at_ref, c_ref, r_ref, d_ref, base_ref, next_hbm, sum_hbm, next_buf, sum_buf, sem
):
    planes, rows, _ = d_ref.shape
    wide_m, wide_b = spread_ref.shape[0], row_at_ref.shape[0]
    ring, part = next_buf.shape[0], next_buf.shape[1]
    spread = spread_ref[...].astype(bf16)
    row_at = row_at_ref[...]

    def copies(n):
        at = pl.ds(n % cuts * part, part)
        slot = n % ring
        return (
            pltpu.make_async_copy(next_buf.at[slot], next_hbm.at[n // cuts, at], sem.at[0, slot]),
            pltpu.make_async_copy(sum_buf.at[slot], sum_hbm.at[n // cuts, at], sem.at[1, slot]),
        )

    for p in range(planes):
        col = c_ref[p * wide_m : (p + 1) * wide_m, :]
        col_hi = col.astype(bf16).astype(f32)
        left = jnp.concatenate([col_hi, col - col_hi, row_at, row_at], axis=0)
        left = jnp.transpose(left).astype(bf16)
        row_hi, row_lo = split(r_ref[p * wide_b : (p + 1) * wide_b, :])
        right = jnp.concatenate([spread, spread, row_hi, row_lo], axis=0)
        for q in range(cuts):
            n = p * cuts + q
            slot = n % ring
            if n >= ring:
                for copy in copies(n - ring):
                    copy.wait()
            at = slice(q * part, (q + 1) * part)
            slope_next = d_ref[p, at, :] + mm(left[at], right)
            next_buf[slot] = slope_next
            sum_buf[slot] = base_ref[p, at, :] + step_size / 3.0 * slope_next
            for copy in copies(n):
                copy.start()
    for n in range(planes * cuts - ring, planes * cuts):
        for copy in copies(n):
            copy.wait()


def order(layers, layer):
    table = [
        sorted(range(layers), key=lambda n: (n == at, n > at, abs(n - at))) for at in range(layers)
    ]
    result = []
    for n in range(layers):
        value = table[0][n]
        for at in range(1, layers):
            value = jnp.where(layer == at, table[at][n], value)
        result.append(value)
    return result


def layer_size(mesh):
    tiers = mesh.shape["tier"]
    devices = mesh.devices[:, 0]
    if not hasattr(devices[0], "coords"):
        return tiers
    places = [tuple(device.coords) for device in devices]
    runs = [
        1 + sum(a[axis] != b[axis] for a, b in zip(places, places[1:]))
        for axis in range(len(places[0]))
    ]
    return tiers // min(count for count in runs + [tiers] if count > 1)


def shards(tiers, systems, group, state, slope, counts, links, mode_site, mode_coef, mode_rate, h_bands):
    slots, _, rows, levels = state.shape
    edge = h_bands.shape[0] - 1
    modes = mode_site.shape[0]
    block = modes // systems
    per_slot = links.shape[2]
    total = slots * per_slot
    cp = total // tiers
    rp = 2 * -(-(slots * block) // tiers)
    parts = 2 * rows // 128
    packet = up(cp * parts, 8)
    cj, rw = packet // parts, up(2 * rp, 8)
    wide_m, wide_b = up(modes, 16), up(block, 16)
    arrays = (links, counts, mode_site, mode_coef, mode_rate, h_bands, state, slope)
    vmem = pl.BlockSpec(memory_space=pltpu.VMEM)
    hbm = pl.BlockSpec(memory_space=pltpu.HBM)
    planes = slots * 2
    wide_rp = up(2 * slots * block, 128)
    dma = pltpu.SemaphoreType.DMA
    big = (planes, rows, levels)
    width = 256 if levels % 256 == 0 else levels
    deriv, base, col_mix, row_mix, spread, row_at = pl.pallas_call(
        functools.partial(
            exchange_kernel, (tiers, systems, group, slots, modes, block, edge, per_slot, rp, cj, rw)
        ),
        out_shape=(
            pltpu.VMEM(big, f32),
            pltpu.VMEM(big, f32),
            pltpu.VMEM((planes * wide_m, rows), f32),
            pltpu.VMEM((planes * wide_b, levels), f32),
            pltpu.VMEM((wide_m, levels), f32),
            pltpu.VMEM((wide_b, rows), f32),
        ),
        in_specs=[hbm] * 8,
        out_specs=(vmem,) * 6,
        scratch_shapes=[
            pltpu.VMEM(links.shape, jnp.int32),
            pltpu.SMEM(counts.shape, jnp.int32),
            pltpu.SMEM(mode_site.shape, jnp.int32),
            pltpu.SMEM(mode_coef.shape, f32),
            pltpu.SMEM(mode_rate.shape, f32),
            pltpu.VMEM(h_bands.shape, f32),
            (pltpu.VMEM((rows, levels), f32),) * planes,
            (pltpu.VMEM((rows, levels), f32),) * planes,
            pltpu.VMEM((planes, rows, levels), bf16),
            pltpu.VMEM((planes, rows, levels), bf16),
            pltpu.VMEM((levels // width, width, width), bf16),
            pltpu.VMEM((levels // width, width, width), bf16),
            pltpu.VMEM((tiers, 1, 128), f32),
            pltpu.VMEM((tiers, 1, 128), f32),
            pltpu.VMEM((2, planes, edge, levels), f32),
            pltpu.VMEM((2, planes, edge, levels), f32),
            pltpu.VMEM((2 * (levels // width), 128, width), bf16),
            pltpu.VMEM((2 * (levels // width), 128, width), bf16),
            pltpu.VMEM((parts, slots * wide_m, 128), bf16),
            pltpu.VMEM((parts, slots * wide_m, 128), bf16),
            pltpu.VMEM((wide_rp, levels), f32),
            pltpu.VMEM((tiers * rw, levels + packet * 16), f32),
            pltpu.VMEM((tiers * rw, levels + packet * 16), f32),
            dma((2, planes)),
            dma((tiers,)),
            dma((tiers,)),
            dma((2,)),
            dma((2,)),
            dma((tiers,)),
            dma((tiers,)),
            dma((6,)),
            pltpu.SemaphoreType.REGULAR((tiers // group,)),
            pltpu.SemaphoreType.REGULAR,
        ],
        compiler_params=pltpu.CompilerParams(
            collective_id=0, has_side_effects=True, vmem_limit_bytes=32 << 20
        ),
        name="exchange",
    )(*(pltpu.with_memory_space_constraint(x, pltpu.HBM) for x in arrays))
    cuts, ring = 2, 8
    outs = pl.pallas_call(
        functools.partial(finish_kernel, cuts),
        out_shape=(jax.ShapeDtypeStruct(big, f32),) * 2,
        in_specs=[vmem] * 6,
        out_specs=(hbm, hbm),
        scratch_shapes=[
            pltpu.VMEM((ring, rows // cuts, levels), f32),
            pltpu.VMEM((ring, rows // cuts, levels), f32),
            dma((2, ring)),
        ],
        compiler_params=pltpu.CompilerParams(vmem_limit_bytes=16 << 20),
        name="finish",
    )(spread, row_at, col_mix, row_mix, deriv, base)
    return tuple(out.reshape(state.shape) for out in outs)


def solution(mesh):
    in_specs = (
        P("tier", None, "sys", None),
        P("tier", None, "sys", None),
        P(),
        P(None, "tier", None),
        P(),
        P(),
        P(),
        P(),
    )
    out_specs = (P("tier", None, "sys", None), P("tier", None, "sys", None))
    body = functools.partial(shards, mesh.shape["tier"], mesh.shape["sys"], layer_size(mesh))
    return jax.shard_map(body, mesh=mesh, in_specs=in_specs, out_specs=out_specs, check_vma=False)
```

```python
import functools

import jax
import jax.numpy as jnp
from jax import lax
from jax.experimental import pallas as pl
from jax.experimental.pallas import tpu as pltpu
from jax.sharding import PartitionSpec as P

step_size = 0.05
MESH = pl.DeviceIdType.MESH
f32 = jnp.float32
bf16 = jnp.bfloat16


def up(value, unit):
    return (value + unit - 1) // unit * unit


def split(value):
    hi = value.astype(bf16)
    lo = (value - hi.astype(f32)).astype(bf16)
    return hi, lo


def mm(a, b):
    return lax.dot_general(a, b, (((1,), (0,)), ((), ())), preferred_element_type=f32)


def mm_nt(a, b):
    return lax.dot_general(a, b, (((1,), (1,)), ((), ())), preferred_element_type=f32)


def mm3(a, b):
    a_hi, a_lo = split(a)
    b_hi, b_lo = split(b)
    return mm(a_hi, b_hi) + (mm(a_hi, b_lo) + mm(a_lo, b_hi))


def exchange_kernel(
    dims,
    links_hbm,
    counts_hbm,
    site_hbm,
    coef_hbm,
    rate_hbm,
    bands_hbm,
    state_hbm,
    slope_hbm,
    d_buf,
    base_ref,
    c_ref,
    r_ref,
    spread_ref,
    row_at_ref,
    links_ref,
    counts_ref,
    site_ref,
    coef_ref,
    rate_ref,
    bands_ref,
    st,
    sl,
    z_hi,
    z_lo,
    h_hi,
    h_lo,
    req_ref,
    req_in,
    halo_out,
    halo_in,
    cross_hi,
    cross_lo,
    col_hi,
    col_lo,
    row_pack,
    send_buf,
    recv_buf,
    load_sem,
    req_send,
    req_recv,
    halo_send,
    halo_recv,
    pack_send,
    pack_recv,
    small_sem,
    here_sem,
    near_sem,
):
    tiers, systems, group, slots, modes, block, edge, per_slot, rp, cj, rw = dims
    rows, levels = st[0].shape
    me = lax.axis_index("tier")
    sy = lax.axis_index("sys")
    planes = slots * 2
    layers = tiers // group
    layer = me // group
    wide_m = spread_ref.shape[0]
    parts = 2 * rows // 128
    per_tile = 8 // parts
    tiles = cj // per_tile
    visits = order(layers, layer)
    place_in = me - layer * group
    first = layer * group

    def load(p):
        g, c = p // 2, p % 2
        return (
            pltpu.make_async_copy(state_hbm.at[g, c], st[p], load_sem.at[0, p]),
            pltpu.make_async_copy(slope_hbm.at[g, c], sl[p], load_sem.at[1, p]),
        )

    small = [
        pltpu.make_async_copy(src, dst, small_sem.at[n])
        for n, (src, dst) in enumerate(
            (
                (links_hbm, links_ref),
                (counts_hbm, counts_ref),
                (site_hbm, site_ref),
                (coef_hbm, coef_ref),
                (rate_hbm, rate_ref),
                (bands_hbm, bands_ref),
            )
        )
    ]
    for copy in small:
        copy.start()

    barrier = pltpu.get_barrier_semaphore()

    turns = [lax.rem(place_in + i, group) for i in range(group)]

    def greet(t):
        pl.semaphore_signal(barrier, inc=1, device_id=(t, sy), device_id_type=MESH)

    def mates(act):
        for i in range(1, group):
            act(first + turns[i])

    def layer_at(step, act):
        @pl.when((layer + step >= 0) & (layer + step < layers))
        def _():
            for i in range(group):
                act((layer + step) * group + turns[i])

    mates(greet)
    for step in range(1, layers):
        layer_at(step, greet)

    @pl.when(sy < systems - 1)
    def _():
        pl.semaphore_signal(barrier, inc=1, device_id=(me, sy + 1), device_id_type=MESH)

    for p in range(planes):
        for copy in load(p):
            copy.start()

    def announce(t):
        pl.semaphore_signal(here_sem.at[layer], inc=1, device_id=(t, sy), device_id_type=MESH)

    pl.semaphore_wait(barrier, first + group - 1 + (sy > 0).astype(jnp.int32))
    for step in range(layers - 1, 0, -1):
        layer_at(-step, announce)

    @pl.when(sy > 0)
    def _():
        pl.semaphore_signal(near_sem, inc=1, device_id=(me, sy - 1), device_id_type=MESH)

    total = slots * per_slot
    wide_q = up(total, 128)

    def iota(shape, axis):
        return lax.broadcasted_iota(jnp.int32, shape, axis).astype(f32)

    def flag(where):
        return jnp.where(where, 1.0, 0.0)

    for copy in small:
        copy.wait()
    flat = jnp.zeros((4, wide_q), f32)
    for g in range(slots):
        place = flag(
            iota((per_slot, wide_q), 1) == iota((per_slot, wide_q), 0) + float(g * per_slot)
        )
        flat += mm(links_ref[:, g, :].astype(f32).astype(bf16), place.astype(bf16))
    lane_q = iota((1, wide_q), 1)
    valid = lane_q < float(total)
    mode, kind, level = flat[1:2], flat[2:3], flat[3:4]
    holder = jnp.floor((flat[0:1] + 0.5) * (1.0 / slots))
    target = flat[0:1] - holder * float(slots)
    holder = jnp.where(valid, holder, -1.0)
    slot_of = jnp.where(valid, jnp.floor((lane_q + 0.5) * (1.0 / per_slot)), -1.0)
    first_mode = (sy * block).astype(f32)
    in_block = valid & (mode >= first_mode) & (mode < first_mode + float(block))
    local_mode = mode - first_mode
    has = flag(holder == iota((tiers, wide_q), 0))
    has_r = has * flag(in_block)
    before = flag(iota((wide_q, wide_q), 0) < iota((wide_q, wide_q), 1)).astype(bf16)
    rank_c = jnp.sum(has * mm(has.astype(bf16), before), axis=0, keepdims=True)
    rank_r = jnp.sum(has_r * mm(has_r.astype(bf16), before), axis=0, keepdims=True)
    lane_j = iota((128, wide_q), 0)

    def asked(codes, ranks):
        return mm_nt(codes.astype(bf16), flag(lane_j == ranks).astype(bf16))

    req = asked(has * (target * float(wide_m) + mode + 1.0), rank_c) - 1.0
    for c in range(2):
        code = (target + float(c * slots)) * float(block) + local_mode + 1.0
        req += asked(has_r * code, rank_r + float(8 + c * rp))
    for t in range(tiers):
        req_ref[t] = req[t : t + 1, :]
    req_in[me] = req_ref[me]

    def request(t, other):
        return pltpu.make_async_remote_copy(
            src_ref=req_ref.at[t],
            dst_ref=req_in.at[other],
            send_sem=req_send.at[t],
            recv_sem=req_recv.at[other],
            device_id=(t, sy),
            device_id_type=MESH,
        )

    def ask(t):
        request(t, me).start()

    for step in range(layers - 1, 0, -1):
        layer_at(-step, ask)
    mates(ask)

    def ask_above(step):
        @pl.when(layer + step < layers)
        def _():
            pl.semaphore_wait(here_sem.at[layer + step], group)

        layer_at(step, ask)

    for step in range(1, layers):
        ask_above(step)

    row_pack[...] = jnp.zeros_like(row_pack)
    col_hi[...] = jnp.zeros_like(col_hi)
    col_lo[...] = jnp.zeros_like(col_lo)
    site_lane = lax.broadcasted_iota(jnp.int32, (1, levels), 1)
    spread_ref[...] = jnp.zeros_like(spread_ref)
    for k in range(modes):
        spread_ref[k : k + 1, :] = flag(site_lane == site_ref[k])
    pick = spread_ref[...].astype(bf16)
    for g in range(slots):
        for c in range(2):
            p = g * 2 + c
            for copy in load(p):
                copy.wait()
            mid = st[p][...] + (0.5 * step_size) * sl[p][...]
            halo_out[0, p] = mid[rows - edge :, :]
            halo_out[1, p] = mid[:edge, :]
            hi, lo = split(mid)
            z_hi[p] = hi
            z_lo[p] = lo
            at = slice(g * wide_m, (g + 1) * wide_m)
            for dest, part in ((col_hi, hi), (col_lo, lo)):
                cols = mm_nt(pick, part).astype(bf16)
                for h in range(-(-rows // 128)):
                    q = c * rows // 128 + h
                    lane = c * rows % 128
                    dest[q, at, lane : lane + min(rows, 128)] = cols[:, h * 128 : h * 128 + 128]
            for k in range(block):
                at = jnp.clip(site_ref[sy * block + k] - sy * rows, 0, rows - 1)
                row = st[p][pl.ds(at, 1), :] + (0.5 * step_size) * sl[p][pl.ds(at, 1), :]
                dest = (c * slots + g) * block + k
                row_pack[dest : dest + 1, :] = row

    def halo(side):
        return pltpu.make_async_remote_copy(
            src_ref=halo_out.at[side],
            dst_ref=halo_in.at[side],
            send_sem=halo_send.at[side],
            recv_sem=halo_recv.at[side],
            device_id=(me, sy + 1 if side == 0 else sy - 1),
            device_id_type=MESH,
        )

    @pl.when(sy > 0)
    def _():
        halo(1).start()

    @pl.when(sy < systems - 1)
    def _():
        pl.semaphore_wait(near_sem, 1)
        halo(0).start()

    @pl.when(sy == 0)
    def _():
        halo_in[0] = jnp.zeros_like(halo_in[0])

    @pl.when(sy == systems - 1)
    def _():
        halo_in[1] = jnp.zeros_like(halo_in[1])

    def pack(n, turn, t, other):
        at = pl.multiple_of((n * group + turn) * rw, rw)
        return pltpu.make_async_remote_copy(
            src_ref=send_buf.at[pl.ds(at, rw), :],
            dst_ref=recv_buf.at[pl.ds(pl.multiple_of(other * rw, rw), rw), :],
            send_sem=pack_send.at[n * group + turn],
            recv_sem=pack_recv.at[other],
            device_id=(t, sy),
            device_id_type=MESH,
        )

    def calls(act):
        for n in range(layers):
            for i in range(1 if n == layers - 1 else 0, group):
                act(n, turns[i], visits[n] * group + turns[i])

    row_hi, row_lo = split(row_pack[...])
    per_c, per_r = tiles * group * 8, group * rw
    index = iota((per_c, 128), 0)
    tile = jnp.floor((index + 0.5) * (1.0 / (group * 8)))
    index -= tile * float(group * 8)
    owner = jnp.floor((index + 0.5) * (1.0 / 8))
    index -= owner * 8.0
    column = jnp.floor((index + 0.5) * (1.0 / parts))
    part_of = index - column * float(parts)
    wanted = tile * float(per_tile) + column
    index = iota((per_r, 128), 0)
    owner_r = jnp.floor((index + 0.5) * (1.0 / rw))
    wanted_r = index - owner_r * float(rw) + 8.0
    owner = jnp.concatenate([owner, owner_r], axis=0)
    spot = flag(jnp.concatenate([wanted, wanted_r], axis=0) == iota((per_c + per_r, 128), 1))
    expand = flag(owner[:, 0:1] == iota((per_c + per_r, group), 1)).astype(bf16)
    wide_k = parts * slots * wide_m
    wanted_at = iota((per_c, wide_k), 1) - part_of[:, 0:1] * float(slots * wide_m)
    in_part = (wanted_at >= 0.0) & (wanted_at < float(slots * wide_m))
    wanted_at = jnp.where(in_part, wanted_at, -2.0)
    wanted_row = iota((per_r, row_pack.shape[0]), 1)
    for n in range(layers):
        start = visits[n] * group
        for i in range(1 if n == layers - 1 else 0, group):
            request(start + turns[i], start + turns[i]).wait_recv()
        codes = mm(expand, req_in[pl.ds(start, group), 0, :].astype(bf16))
        code = jnp.sum(codes * spot, axis=1, keepdims=True)
        pick_c = flag(code[:per_c] == wanted_at).astype(bf16)
        pick_r = flag(code[per_c:] == wanted_row).astype(bf16)
        packed = mm(pick_c, col_hi[...].reshape(wide_k, 128)) + mm(
            pick_c, col_lo[...].reshape(wide_k, 128)
        )
        here = slice(n * group * rw, (n + 1) * group * rw)
        send_buf[here, 0:levels] = mm(pick_r, row_hi) + mm(pick_r, row_lo)
        for k in range(tiles):
            send_buf[here, levels + k * 128 : levels + (k + 1) * 128] = packed[
                k * group * 8 : (k + 1) * group * 8
            ]
        for i in range(1 if n == layers - 1 else 0, group):
            pack(n, turns[i], start + turns[i], me).start()
    own = pl.multiple_of(((layers - 1) * group + place_in) * rw, rw)
    recv_buf[pl.ds(pl.multiple_of(me * rw, rw), rw), :] = send_buf[pl.ds(own, rw), :]

    row_start = sy * rows
    blocks = levels // 128
    over = h_hi.shape[1] // 128
    diff = lax.broadcasted_iota(jnp.int32, (128, 128), 0) - lax.broadcasted_iota(
        jnp.int32, (128, 128), 1
    )
    bands = bands_ref[...]
    moved = [bands[o : o + 1, :] if o == 0 else pltpu.roll(bands, o, 1)[o : o + 1, :] for o in range(edge + 1)]

    def block_of(row, b):
        return row[:, b * 128 : (b + 1) * 128]

    def keep(hi_ref, lo_ref, n, row, lane, value):
        hi, lo = split(-value)
        high, wide = value.shape
        hi_ref[n, row : row + high, lane : lane + wide] = hi
        lo_ref[n, row : row + high, lane : lane + wide] = lo

    for ref in (h_hi, h_lo, cross_hi, cross_lo):
        ref[...] = jnp.zeros_like(ref)
    for b in range(blocks):
        value = jnp.where(diff == 0, block_of(bands[0:1, :], b), 0.0)
        for o in range(1, edge + 1):
            value = jnp.where(diff == o, block_of(bands[o : o + 1, :], b), value)
            value = jnp.where(diff == -o, block_of(moved[o], b), value)
        n, at = b // over, b % over * 128
        keep(h_hi, h_lo, n, at, at, value)
    corner = 2 * edge
    slant = diff[0:corner, :]
    for b in range(blocks - 1):
        above = jnp.zeros((corner, 128), f32)
        below = jnp.zeros((corner, 128), f32)
        for o in range(1, edge + 1):
            above = jnp.where(slant == corner - o, block_of(moved[o], b + 1), above)
            below = jnp.where(slant == o - 128, block_of(bands[o : o + 1, :], b), below)
        n, at = b // over, b % over * 128
        if b % over < over - 1:
            keep(h_hi, h_lo, n, at + 128 - corner, at + 128, above)
            keep(h_hi, h_lo, n, at + 128, at, below)
        else:
            keep(cross_hi, cross_lo, 2 * n, 0, at, below)
            keep(cross_hi, cross_lo, 2 * n + 1, 128 - corner, 0, above)

    def rolled(shift):
        return pltpu.roll(bands, lax.rem(shift + 2 * levels, levels), 1)

    if rows == h_hi.shape[1]:
        loc_hi, loc_lo = -h_hi[sy], -h_lo[sy]
    else:
        wide_r = up(rows, 128)
        gap = lax.broadcasted_iota(jnp.int32, (rows, wide_r), 0) - lax.broadcasted_iota(
            jnp.int32, (rows, wide_r), 1
        )
        near_bands = rolled(-row_start)
        loc = jnp.where(gap == 0, near_bands[0:1, :wide_r], 0.0)
        for o in range(1, edge + 1):
            loc = jnp.where(gap == o, near_bands[o : o + 1, :wide_r], loc)
            loc = jnp.where(gap == -o, pltpu.roll(near_bands, o, 1)[o : o + 1, :wide_r], loc)
        loc_hi, loc_lo = split(loc[:, :rows])
    sub = lax.broadcasted_iota(jnp.int32, (2 * edge, 128), 0)
    lan = lax.broadcasted_iota(jnp.int32, (2 * edge, 128), 1)
    low_bands = rolled(edge - row_start)
    high_bands = rolled(edge - row_start - rows)
    halo_h = jnp.zeros((2 * edge, 128), f32)
    for o in range(edge + 1):
        low = (sub < edge) & (lan < edge) & (edge + sub - lan == o)
        high = (sub >= edge) & (lan >= edge) & (lan < 2 * edge) & (edge + lan - sub == o)
        above = pltpu.roll(high_bands, o, 1) if o else high_bands
        halo_h = jnp.where(low, low_bands[o : o + 1, :128], halo_h)
        halo_h = jnp.where(high, above[o : o + 1, :128], halo_h)
    ghost_hi, ghost_lo = split(halo_h)
    ghost_h = jnp.where(lan < 2 * edge, ghost_hi.astype(f32), 0.0)
    ghost_h += pltpu.roll(jnp.where(lan < 2 * edge, ghost_lo.astype(f32), 0.0), 2 * edge, 1)
    ghost_h += pltpu.roll(jnp.where(lan < 2 * edge, ghost_hi.astype(f32), 0.0), 4 * edge, 1)
    ghost_h = ghost_h.astype(bf16)

    def table(ref, count, index):
        value = jnp.zeros((1, wide_q), f32)
        for k in range(count):
            value = jnp.where(index == float(k), ref(k), value)
        return value

    own_count = counts_ref[me].astype(f32)
    near = flag(target < table(lambda k: counts_ref[k].astype(f32), tiers, holder))
    near = near * flag(slot_of < own_count)
    down = kind == 1.0
    w_re = jnp.where(down, level * table(lambda k: coef_ref[0, k], modes, mode), 1.0) * near
    w_im = jnp.where(down, level * table(lambda k: coef_ref[1, k], modes, mode), 0.0) * near
    rate = jnp.where(down, level * table(lambda k: rate_ref[k], modes, mode), 0.0)
    wide_b = row_at_ref.shape[0]

    def mixing(wide, index, mask, signs):
        from_re, from_im = [], []
        for g in range(slots):
            own = flag((iota((wide, wide_q), 0) == index) & (slot_of == float(g)) & mask)
            for re, im in signs:
                from_re.append(own * re)
                from_im.append(own * im)
        return jnp.concatenate(from_re, axis=0), jnp.concatenate(from_im, axis=0)

    def packets(count, at, mask):
        return flag((iota((count, wide_q), 0) == at) & mask).astype(bf16)

    def place(value, at):
        hi, lo = split(value)
        return mm_nt(hi, at) + mm_nt(lo, at)

    rank_tile = jnp.floor((rank_c + 0.5) * (1.0 / per_tile))
    at_tile = rank_tile * float(tiers * 8) + holder * 8.0
    at_tile += (rank_c - rank_tile * float(per_tile)) * float(parts)
    from_re, from_im = mixing(wide_m, mode, valid, ((w_im, -w_re), (w_re, w_im)))

    def column_mix(value, q):
        return place(value, packets(tiles * tiers * 8, at_tile + float(q), valid))

    if rows < 128:
        mix_c = [column_mix(from_re, 0), column_mix(from_im, 0)]
    else:
        mix_c = [
            column_mix(from_re, h) + column_mix(from_im, parts // 2 + h) for h in range(parts // 2)
        ]
    from_re, from_im = mixing(wide_b, local_mode, in_block, ((w_im, w_re), (-w_re, w_im)))
    at_row = holder * float(rw) + rank_r
    mix_r = place(from_re, packets(tiers * rw, at_row, in_block)) + place(
        from_im, packets(tiers * rw, at_row + float(rp), in_block)
    )
    row_lane = lax.broadcasted_iota(jnp.int32, (1, rows), 1)
    row_at_ref[...] = jnp.zeros_like(row_at_ref)
    for k in range(block):
        row_at_ref[k : k + 1, :] = flag(row_lane == site_ref[sy * block + k] - row_start)

    def dots(pairs):
        if rows % 128 == 0:
            return mm(
                jnp.concatenate([a for a, _ in pairs], axis=1),
                jnp.concatenate([b for _, b in pairs], axis=0),
            )
        return sum(mm(a, b) for a, b in pairs)

    width = h_hi.shape[1]
    cuts = levels // width

    def commute(p, n):
        hi, lo = z_hi.at[p], z_lo.at[p]
        at = slice(n * width, (n + 1) * width)
        near_hi, near_lo = hi[:, at], lo[:, at]
        pairs = [(loc_hi, near_hi), (loc_lo, near_hi), (loc_hi, near_lo)]
        pairs += [(near_hi, h_hi[n]), (near_hi, h_lo[n]), (near_lo, h_hi[n])]
        for side, there in ((2 * n, (n + 1) * width), (2 * n - 1, n * width - 128)):
            if 0 <= side < 2 * (cuts - 1):
                there = slice(there, there + 128)
                pairs += [(hi[:, there], cross_hi[side]), (hi[:, there], cross_lo[side])]
                pairs += [(lo[:, there], cross_hi[side])]
        return dots(pairs)

    def ghost(p):
        hi, lo = split(jnp.concatenate([halo_in[s, p] for s in range(2)], axis=0))
        rest = jnp.zeros((128 - 6 * edge, levels), bf16)
        return mm(ghost_h, jnp.concatenate([hi, hi, lo, rest], axis=0))

    for g in range(slots):
        live = flag(own_count > float(g))
        damp = jnp.sum(jnp.where(slot_of == float(g), rate, 0.0), axis=1, keepdims=True) * live
        for c in range(2):
            p = g * 2 + c
            sign = live if c == 0 else -live
            for n in range(cuts):
                at = slice(n * width, (n + 1) * width)
                mid = st[p][:, at] + (0.5 * step_size) * sl[p][:, at]
                d_buf[p, :, at] = sign * commute(g * 2 + 1 - c, n) - damp * mid
                base_ref[p, :, at] = live * (st[p][:, at] + (step_size / 6.0) * sl[p][:, at])

    @pl.when(sy > 0)
    def _():
        halo(0).wait_recv()

    @pl.when(sy < systems - 1)
    def _():
        halo(1).wait_recv()

    for g in range(slots):
        live = flag(own_count > float(g))
        for c in range(2):
            extra = (live if c == 0 else -live) * ghost(g * 2 + 1 - c)
            d_buf[g * 2 + c, 0:edge, :] += extra[0:edge]
            d_buf[g * 2 + c, rows - edge : rows, :] += extra[edge : 2 * edge]

    calls(lambda n, turn, t: request(t, me).wait_send())
    calls(lambda n, turn, t: pack(n, turn, t, me).wait_send())

    @pl.when(sy < systems - 1)
    def _():
        halo(0).wait_send()

    @pl.when(sy > 0)
    def _():
        halo(1).wait_send()

    calls(lambda n, turn, t: pack(n, turn, t, t).wait_recv())
    got_c = jnp.concatenate(
        [recv_buf[:, levels + n * 128 : levels + (n + 1) * 128] for n in range(tiles)], axis=0
    )
    got_r = recv_buf[:, 0:levels]
    r_ref[...] = mm3(mix_r, got_r)
    if rows < 128:
        c_ref[...] = mm3(mix_c[0], got_c[:, :rows]) + mm3(mix_c[1], got_c[:, rows:])
    else:
        for h in range(parts // 2):
            c_ref[:, h * 128 : (h + 1) * 128] = mm3(mix_c[h], got_c)


def finish_kernel(
    cuts, spread_ref, row_at_ref, c_ref, r_ref, d_ref, base_ref, next_hbm, sum_hbm, next_buf, sum_buf, sem
):
    planes, rows, _ = d_ref.shape
    wide_m, wide_b = spread_ref.shape[0], row_at_ref.shape[0]
    ring, part = next_buf.shape[0], next_buf.shape[1]
    spread = spread_ref[...].astype(bf16)
    row_at = row_at_ref[...]

    def copies(n):
        at = pl.ds(n % cuts * part, part)
        slot = n % ring
        return (
            pltpu.make_async_copy(next_buf.at[slot], next_hbm.at[n // cuts, at], sem.at[0, slot]),
            pltpu.make_async_copy(sum_buf.at[slot], sum_hbm.at[n // cuts, at], sem.at[1, slot]),
        )

    for p in range(planes):
        col = c_ref[p * wide_m : (p + 1) * wide_m, :]
        col_hi = col.astype(bf16).astype(f32)
        left = jnp.concatenate([col_hi, col - col_hi, row_at, row_at], axis=0)
        left = jnp.transpose(left).astype(bf16)
        row_hi, row_lo = split(r_ref[p * wide_b : (p + 1) * wide_b, :])
        right = jnp.concatenate([spread, spread, row_hi, row_lo], axis=0)
        for q in range(cuts):
            n = p * cuts + q
            slot = n % ring
            if n >= ring:
                for copy in copies(n - ring):
                    copy.wait()
            at = slice(q * part, (q + 1) * part)
            slope_next = d_ref[p, at, :] + mm(left[at], right)
            next_buf[slot] = slope_next
            sum_buf[slot] = base_ref[p, at, :] + step_size / 3.0 * slope_next
            for copy in copies(n):
                copy.start()
    for n in range(planes * cuts - ring, planes * cuts):
        for copy in copies(n):
            copy.wait()


def order(layers, layer):
    table = [
        sorted(range(layers), key=lambda n: (n == at, -abs(n - at), n)) for at in range(layers)
    ]
    result = []
    for n in range(layers):
        value = table[0][n]
        for at in range(1, layers):
            value = jnp.where(layer == at, table[at][n], value)
        result.append(value)
    return result


def layer_size(mesh):
    tiers = mesh.shape["tier"]
    devices = mesh.devices[:, 0]
    if not hasattr(devices[0], "coords"):
        return tiers
    places = [tuple(device.coords) for device in devices]
    runs = [
        1 + sum(a[axis] != b[axis] for a, b in zip(places, places[1:]))
        for axis in range(len(places[0]))
    ]
    return tiers // min(count for count in runs + [tiers] if count > 1)


def shards(tiers, systems, group, state, slope, counts, links, mode_site, mode_coef, mode_rate, h_bands):
    slots, _, rows, levels = state.shape
    edge = h_bands.shape[0] - 1
    modes = mode_site.shape[0]
    block = modes // systems
    per_slot = links.shape[2]
    total = slots * per_slot
    cp = total // tiers
    rp = 2 * -(-(slots * block) // tiers)
    parts = 2 * rows // 128
    packet = up(cp * parts, 8)
    cj, rw = packet // parts, up(2 * rp, 8)
    wide_m, wide_b = up(modes, 16), up(block, 16)
    arrays = (links, counts, mode_site, mode_coef, mode_rate, h_bands, state, slope)
    vmem = pl.BlockSpec(memory_space=pltpu.VMEM)
    hbm = pl.BlockSpec(memory_space=pltpu.HBM)
    planes = slots * 2
    wide_rp = up(2 * slots * block, 128)
    dma = pltpu.SemaphoreType.DMA
    big = (planes, rows, levels)
    width = 256 if levels % 256 == 0 else levels
    deriv, base, col_mix, row_mix, spread, row_at = pl.pallas_call(
        functools.partial(
            exchange_kernel, (tiers, systems, group, slots, modes, block, edge, per_slot, rp, cj, rw)
        ),
        out_shape=(
            pltpu.VMEM(big, f32),
            pltpu.VMEM(big, f32),
            pltpu.VMEM((planes * wide_m, rows), f32),
            pltpu.VMEM((planes * wide_b, levels), f32),
            pltpu.VMEM((wide_m, levels), f32),
            pltpu.VMEM((wide_b, rows), f32),
        ),
        in_specs=[hbm] * 8,
        out_specs=(vmem,) * 6,
        scratch_shapes=[
            pltpu.VMEM(links.shape, jnp.int32),
            pltpu.SMEM(counts.shape, jnp.int32),
            pltpu.SMEM(mode_site.shape, jnp.int32),
            pltpu.SMEM(mode_coef.shape, f32),
            pltpu.SMEM(mode_rate.shape, f32),
            pltpu.VMEM(h_bands.shape, f32),
            (pltpu.VMEM((rows, levels), f32),) * planes,
            (pltpu.VMEM((rows, levels), f32),) * planes,
            pltpu.VMEM((planes, rows, levels), bf16),
            pltpu.VMEM((planes, rows, levels), bf16),
            pltpu.VMEM((levels // width, width, width), bf16),
            pltpu.VMEM((levels // width, width, width), bf16),
            pltpu.VMEM((tiers, 1, 128), f32),
            pltpu.VMEM((tiers, 1, 128), f32),
            pltpu.VMEM((2, planes, edge, levels), f32),
            pltpu.VMEM((2, planes, edge, levels), f32),
            pltpu.VMEM((2 * (levels // width), 128, width), bf16),
            pltpu.VMEM((2 * (levels // width), 128, width), bf16),
            pltpu.VMEM((parts, slots * wide_m, 128), bf16),
            pltpu.VMEM((parts, slots * wide_m, 128), bf16),
            pltpu.VMEM((wide_rp, levels), f32),
            pltpu.VMEM((tiers * rw, levels + packet * 16), f32),
            pltpu.VMEM((tiers * rw, levels + packet * 16), f32),
            dma((2, planes)),
            dma((tiers,)),
            dma((tiers,)),
            dma((2,)),
            dma((2,)),
            dma((tiers,)),
            dma((tiers,)),
            dma((6,)),
            pltpu.SemaphoreType.REGULAR((tiers // group,)),
            pltpu.SemaphoreType.REGULAR,
        ],
        compiler_params=pltpu.CompilerParams(
            collective_id=0, has_side_effects=True, vmem_limit_bytes=32 << 20
        ),
        name="exchange",
    )(*(pltpu.with_memory_space_constraint(x, pltpu.HBM) for x in arrays))
    cuts, ring = 2, 8
    outs = pl.pallas_call(
        functools.partial(finish_kernel, cuts),
        out_shape=(jax.ShapeDtypeStruct(big, f32),) * 2,
        in_specs=[vmem] * 6,
        out_specs=(hbm, hbm),
        scratch_shapes=[
            pltpu.VMEM((ring, rows // cuts, levels), f32),
            pltpu.VMEM((ring, rows // cuts, levels), f32),
            dma((2, ring)),
        ],
        compiler_params=pltpu.CompilerParams(vmem_limit_bytes=16 << 20),
        name="finish",
    )(spread, row_at, col_mix, row_mix, deriv, base)
    return tuple(out.reshape(state.shape) for out in outs)


def solution(mesh):
    in_specs = (
        P("tier", None, "sys", None),
        P("tier", None, "sys", None),
        P(),
        P(None, "tier", None),
        P(),
        P(),
        P(),
        P(),
    )
    out_specs = (P("tier", None, "sys", None), P("tier", None, "sys", None))
    body = functools.partial(shards, mesh.shape["tier"], mesh.shape["sys"], layer_size(mesh))
    return jax.shard_map(body, mesh=mesh, in_specs=in_specs, out_specs=out_specs, check_vma=False)
```

```python
import functools

import jax
import jax.numpy as jnp
from jax import lax
from jax.experimental import pallas as pl
from jax.experimental.pallas import tpu as pltpu
from jax.sharding import PartitionSpec as P

step_size = 0.05
MESH = pl.DeviceIdType.MESH
f32 = jnp.float32
bf16 = jnp.bfloat16


def up(value, unit):
    return (value + unit - 1) // unit * unit


def split(value):
    hi = value.astype(bf16)
    lo = (value - hi.astype(f32)).astype(bf16)
    return hi, lo


def mm(a, b):
    return lax.dot_general(a, b, (((1,), (0,)), ((), ())), preferred_element_type=f32)


def mm_nt(a, b):
    return lax.dot_general(a, b, (((1,), (1,)), ((), ())), preferred_element_type=f32)


def mm3(a, b):
    a_hi, a_lo = split(a)
    b_hi, b_lo = split(b)
    return mm(a_hi, b_hi) + (mm(a_hi, b_lo) + mm(a_lo, b_hi))


def exchange_kernel(
    dims,
    links_hbm,
    counts_hbm,
    site_hbm,
    coef_hbm,
    rate_hbm,
    bands_hbm,
    state_hbm,
    slope_hbm,
    d_buf,
    base_ref,
    c_ref,
    r_ref,
    spread_ref,
    row_at_ref,
    links_ref,
    counts_ref,
    site_ref,
    coef_ref,
    rate_ref,
    bands_ref,
    st,
    sl,
    z_hi,
    z_lo,
    h_hi,
    h_lo,
    req_ref,
    req_in,
    halo_out,
    halo_in,
    cross_hi,
    cross_lo,
    col_hi,
    col_lo,
    row_pack,
    send_buf,
    recv_buf,
    load_sem,
    req_send,
    req_recv,
    halo_send,
    halo_recv,
    pack_send,
    pack_recv,
    small_sem,
    here_sem,
    near_sem,
):
    tiers, systems, group, slots, modes, block, edge, per_slot, rp, cj, rw = dims
    rows, levels = st[0].shape
    me = lax.axis_index("tier")
    sy = lax.axis_index("sys")
    planes = slots * 2
    layers = tiers // group
    layer = me // group
    wide_m = spread_ref.shape[0]
    parts = 2 * rows // 128
    per_tile = 8 // parts
    tiles = cj // per_tile
    visits = order(layers, layer)
    place_in = me - layer * group
    first = layer * group

    def load(p):
        g, c = p // 2, p % 2
        return (
            pltpu.make_async_copy(state_hbm.at[g, c], st[p], load_sem.at[0, p]),
            pltpu.make_async_copy(slope_hbm.at[g, c], sl[p], load_sem.at[1, p]),
        )

    small = [
        pltpu.make_async_copy(src, dst, small_sem.at[n])
        for n, (src, dst) in enumerate(
            (
                (links_hbm, links_ref),
                (counts_hbm, counts_ref),
                (site_hbm, site_ref),
                (coef_hbm, coef_ref),
                (rate_hbm, rate_ref),
                (bands_hbm, bands_ref),
            )
        )
    ]
    for copy in small:
        copy.start()

    barrier = pltpu.get_barrier_semaphore()

    turns = [lax.rem(place_in + i, group) for i in range(group)]

    def greet(t):
        pl.semaphore_signal(barrier, inc=1, device_id=(t, sy), device_id_type=MESH)

    def mates(act):
        for i in range(1, group):
            act(first + turns[i])

    def layer_at(step, act):
        @pl.when((layer + step >= 0) & (layer + step < layers))
        def _():
            for i in range(group):
                act((layer + step) * group + turns[i])

    mates(greet)
    for step in range(1, layers):
        layer_at(step, greet)

    @pl.when(sy < systems - 1)
    def _():
        pl.semaphore_signal(barrier, inc=1, device_id=(me, sy + 1), device_id_type=MESH)

    def announce(t):
        pl.semaphore_signal(here_sem.at[layer], inc=1, device_id=(t, sy), device_id_type=MESH)

    pl.semaphore_wait(barrier, first + group - 1 + (sy > 0).astype(jnp.int32))
    for step in range(layers - 1, 0, -1):
        layer_at(-step, announce)

    @pl.when(sy > 0)
    def _():
        pl.semaphore_signal(near_sem, inc=1, device_id=(me, sy - 1), device_id_type=MESH)

    for p in range(planes):
        for copy in load(p):
            copy.start()

    total = slots * per_slot
    wide_q = up(total, 128)

    def iota(shape, axis):
        return lax.broadcasted_iota(jnp.int32, shape, axis).astype(f32)

    def flag(where):
        return jnp.where(where, 1.0, 0.0)

    for copy in small:
        copy.wait()
    flat = jnp.zeros((4, wide_q), f32)
    for g in range(slots):
        place = flag(
            iota((per_slot, wide_q), 1) == iota((per_slot, wide_q), 0) + float(g * per_slot)
        )
        flat += mm(links_ref[:, g, :].astype(f32).astype(bf16), place.astype(bf16))
    lane_q = iota((1, wide_q), 1)
    valid = lane_q < float(total)
    mode, kind, level = flat[1:2], flat[2:3], flat[3:4]
    holder = jnp.floor((flat[0:1] + 0.5) * (1.0 / slots))
    target = flat[0:1] - holder * float(slots)
    holder = jnp.where(valid, holder, -1.0)
    slot_of = jnp.where(valid, jnp.floor((lane_q + 0.5) * (1.0 / per_slot)), -1.0)
    first_mode = (sy * block).astype(f32)
    in_block = valid & (mode >= first_mode) & (mode < first_mode + float(block))
    local_mode = mode - first_mode
    has = flag(holder == iota((tiers, wide_q), 0))
    has_r = has * flag(in_block)
    before = flag(iota((wide_q, wide_q), 0) < iota((wide_q, wide_q), 1)).astype(bf16)
    rank_c = jnp.sum(has * mm(has.astype(bf16), before), axis=0, keepdims=True)
    rank_r = jnp.sum(has_r * mm(has_r.astype(bf16), before), axis=0, keepdims=True)
    lane_j = iota((128, wide_q), 0)

    def asked(codes, ranks):
        return mm_nt(codes.astype(bf16), flag(lane_j == ranks).astype(bf16))

    req = asked(has * (target * float(wide_m) + mode + 1.0), rank_c) - 1.0
    for c in range(2):
        code = (target + float(c * slots)) * float(block) + local_mode + 1.0
        req += asked(has_r * code, rank_r + float(8 + c * rp))
    for t in range(tiers):
        req_ref[t] = req[t : t + 1, :]
    req_in[me] = req_ref[me]

    def request(t, other):
        return pltpu.make_async_remote_copy(
            src_ref=req_ref.at[t],
            dst_ref=req_in.at[other],
            send_sem=req_send.at[t],
            recv_sem=req_recv.at[other],
            device_id=(t, sy),
            device_id_type=MESH,
        )

    def ask(t):
        request(t, me).start()

    for step in range(layers - 1, 0, -1):
        layer_at(-step, ask)
    mates(ask)

    def ask_above(step):
        @pl.when(layer + step < layers)
        def _():
            pl.semaphore_wait(here_sem.at[layer + step], group)

        layer_at(step, ask)

    for step in range(1, layers):
        ask_above(step)

    row_pack[...] = jnp.zeros_like(row_pack)
    col_hi[...] = jnp.zeros_like(col_hi)
    col_lo[...] = jnp.zeros_like(col_lo)
    site_lane = lax.broadcasted_iota(jnp.int32, (1, levels), 1)
    spread_ref[...] = jnp.zeros_like(spread_ref)
    for k in range(modes):
        spread_ref[k : k + 1, :] = flag(site_lane == site_ref[k])
    pick = spread_ref[...].astype(bf16)
    for g in range(slots):
        for c in range(2):
            p = g * 2 + c
            for copy in load(p):
                copy.wait()
            mid = st[p][...] + (0.5 * step_size) * sl[p][...]
            halo_out[0, p] = mid[rows - edge :, :]
            halo_out[1, p] = mid[:edge, :]
            hi, lo = split(mid)
            z_hi[p] = hi
            z_lo[p] = lo
            at = slice(g * wide_m, (g + 1) * wide_m)
            for dest, part in ((col_hi, hi), (col_lo, lo)):
                cols = mm_nt(pick, part).astype(bf16)
                for h in range(-(-rows // 128)):
                    q = c * rows // 128 + h
                    lane = c * rows % 128
                    dest[q, at, lane : lane + min(rows, 128)] = cols[:, h * 128 : h * 128 + 128]
            for k in range(block):
                at = jnp.clip(site_ref[sy * block + k] - sy * rows, 0, rows - 1)
                row = st[p][pl.ds(at, 1), :] + (0.5 * step_size) * sl[p][pl.ds(at, 1), :]
                dest = (c * slots + g) * block + k
                row_pack[dest : dest + 1, :] = row

    def halo(side):
        return pltpu.make_async_remote_copy(
            src_ref=halo_out.at[side],
            dst_ref=halo_in.at[side],
            send_sem=halo_send.at[side],
            recv_sem=halo_recv.at[side],
            device_id=(me, sy + 1 if side == 0 else sy - 1),
            device_id_type=MESH,
        )

    @pl.when(sy > 0)
    def _():
        halo(1).start()

    @pl.when(sy < systems - 1)
    def _():
        pl.semaphore_wait(near_sem, 1)
        halo(0).start()

    @pl.when(sy == 0)
    def _():
        halo_in[0] = jnp.zeros_like(halo_in[0])

    @pl.when(sy == systems - 1)
    def _():
        halo_in[1] = jnp.zeros_like(halo_in[1])

    def pack(n, turn, t, other):
        at = pl.multiple_of((n * group + turn) * rw, rw)
        return pltpu.make_async_remote_copy(
            src_ref=send_buf.at[pl.ds(at, rw), :],
            dst_ref=recv_buf.at[pl.ds(pl.multiple_of(other * rw, rw), rw), :],
            send_sem=pack_send.at[n * group + turn],
            recv_sem=pack_recv.at[other],
            device_id=(t, sy),
            device_id_type=MESH,
        )

    def calls(act):
        for n in range(layers):
            for i in range(1 if n == layers - 1 else 0, group):
                act(n, turns[i], visits[n] * group + turns[i])

    row_hi, row_lo = split(row_pack[...])
    per_c, per_r = tiles * group * 8, group * rw
    index = iota((per_c, 128), 0)
    tile = jnp.floor((index + 0.5) * (1.0 / (group * 8)))
    index -= tile * float(group * 8)
    owner = jnp.floor((index + 0.5) * (1.0 / 8))
    index -= owner * 8.0
    column = jnp.floor((index + 0.5) * (1.0 / parts))
    part_of = index - column * float(parts)
    wanted = tile * float(per_tile) + column
    index = iota((per_r, 128), 0)
    owner_r = jnp.floor((index + 0.5) * (1.0 / rw))
    wanted_r = index - owner_r * float(rw) + 8.0
    owner = jnp.concatenate([owner, owner_r], axis=0)
    spot = flag(jnp.concatenate([wanted, wanted_r], axis=0) == iota((per_c + per_r, 128), 1))
    expand = flag(owner[:, 0:1] == iota((per_c + per_r, group), 1)).astype(bf16)
    wide_k = parts * slots * wide_m
    wanted_at = iota((per_c, wide_k), 1) - part_of[:, 0:1] * float(slots * wide_m)
    in_part = (wanted_at >= 0.0) & (wanted_at < float(slots * wide_m))
    wanted_at = jnp.where(in_part, wanted_at, -2.0)
    wanted_row = iota((per_r, row_pack.shape[0]), 1)
    for n in range(layers):
        start = visits[n] * group
        for i in range(1 if n == layers - 1 else 0, group):
            request(start + turns[i], start + turns[i]).wait_recv()
        codes = mm(expand, req_in[pl.ds(start, group), 0, :].astype(bf16))
        code = jnp.sum(codes * spot, axis=1, keepdims=True)
        pick_c = flag(code[:per_c] == wanted_at).astype(bf16)
        pick_r = flag(code[per_c:] == wanted_row).astype(bf16)
        packed = mm(pick_c, col_hi[...].reshape(wide_k, 128)) + mm(
            pick_c, col_lo[...].reshape(wide_k, 128)
        )
        here = slice(n * group * rw, (n + 1) * group * rw)
        send_buf[here, 0:levels] = mm(pick_r, row_hi) + mm(pick_r, row_lo)
        for k in range(tiles):
            send_buf[here, levels + k * 128 : levels + (k + 1) * 128] = packed[
                k * group * 8 : (k + 1) * group * 8
            ]
        for i in range(1 if n == layers - 1 else 0, group):
            pack(n, turns[i], start + turns[i], me).start()
    own = pl.multiple_of(((layers - 1) * group + place_in) * rw, rw)
    recv_buf[pl.ds(pl.multiple_of(me * rw, rw), rw), :] = send_buf[pl.ds(own, rw), :]

    row_start = sy * rows
    blocks = levels // 128
    over = h_hi.shape[1] // 128
    diff = lax.broadcasted_iota(jnp.int32, (128, 128), 0) - lax.broadcasted_iota(
        jnp.int32, (128, 128), 1
    )
    bands = bands_ref[...]
    moved = [bands[o : o + 1, :] if o == 0 else pltpu.roll(bands, o, 1)[o : o + 1, :] for o in range(edge + 1)]

    def block_of(row, b):
        return row[:, b * 128 : (b + 1) * 128]

    def keep(hi_ref, lo_ref, n, row, lane, value):
        hi, lo = split(-value)
        high, wide = value.shape
        hi_ref[n, row : row + high, lane : lane + wide] = hi
        lo_ref[n, row : row + high, lane : lane + wide] = lo

    for ref in (h_hi, h_lo, cross_hi, cross_lo):
        ref[...] = jnp.zeros_like(ref)
    for b in range(blocks):
        value = jnp.where(diff == 0, block_of(bands[0:1, :], b), 0.0)
        for o in range(1, edge + 1):
            value = jnp.where(diff == o, block_of(bands[o : o + 1, :], b), value)
            value = jnp.where(diff == -o, block_of(moved[o], b), value)
        n, at = b // over, b % over * 128
        keep(h_hi, h_lo, n, at, at, value)
    corner = 2 * edge
    slant = diff[0:corner, :]
    for b in range(blocks - 1):
        above = jnp.zeros((corner, 128), f32)
        below = jnp.zeros((corner, 128), f32)
        for o in range(1, edge + 1):
            above = jnp.where(slant == corner - o, block_of(moved[o], b + 1), above)
            below = jnp.where(slant == o - 128, block_of(bands[o : o + 1, :], b), below)
        n, at = b // over, b % over * 128
        if b % over < over - 1:
            keep(h_hi, h_lo, n, at + 128 - corner, at + 128, above)
            keep(h_hi, h_lo, n, at + 128, at, below)
        else:
            keep(cross_hi, cross_lo, 2 * n, 0, at, below)
            keep(cross_hi, cross_lo, 2 * n + 1, 128 - corner, 0, above)

    def rolled(shift):
        return pltpu.roll(bands, lax.rem(shift + 2 * levels, levels), 1)

    if rows == h_hi.shape[1]:
        loc_hi, loc_lo = -h_hi[sy], -h_lo[sy]
    else:
        wide_r = up(rows, 128)
        gap = lax.broadcasted_iota(jnp.int32, (rows, wide_r), 0) - lax.broadcasted_iota(
            jnp.int32, (rows, wide_r), 1
        )
        near_bands = rolled(-row_start)
        loc = jnp.where(gap == 0, near_bands[0:1, :wide_r], 0.0)
        for o in range(1, edge + 1):
            loc = jnp.where(gap == o, near_bands[o : o + 1, :wide_r], loc)
            loc = jnp.where(gap == -o, pltpu.roll(near_bands, o, 1)[o : o + 1, :wide_r], loc)
        loc_hi, loc_lo = split(loc[:, :rows])
    sub = lax.broadcasted_iota(jnp.int32, (2 * edge, 128), 0)
    lan = lax.broadcasted_iota(jnp.int32, (2 * edge, 128), 1)
    low_bands = rolled(edge - row_start)
    high_bands = rolled(edge - row_start - rows)
    halo_h = jnp.zeros((2 * edge, 128), f32)
    for o in range(edge + 1):
        low = (sub < edge) & (lan < edge) & (edge + sub - lan == o)
        high = (sub >= edge) & (lan >= edge) & (lan < 2 * edge) & (edge + lan - sub == o)
        above = pltpu.roll(high_bands, o, 1) if o else high_bands
        halo_h = jnp.where(low, low_bands[o : o + 1, :128], halo_h)
        halo_h = jnp.where(high, above[o : o + 1, :128], halo_h)
    ghost_hi, ghost_lo = split(halo_h)
    ghost_h = jnp.where(lan < 2 * edge, ghost_hi.astype(f32), 0.0)
    ghost_h += pltpu.roll(jnp.where(lan < 2 * edge, ghost_lo.astype(f32), 0.0), 2 * edge, 1)
    ghost_h += pltpu.roll(jnp.where(lan < 2 * edge, ghost_hi.astype(f32), 0.0), 4 * edge, 1)
    ghost_h = ghost_h.astype(bf16)

    def table(ref, count, index):
        value = jnp.zeros((1, wide_q), f32)
        for k in range(count):
            value = jnp.where(index == float(k), ref(k), value)
        return value

    own_count = counts_ref[me].astype(f32)
    near = flag(target < table(lambda k: counts_ref[k].astype(f32), tiers, holder))
    near = near * flag(slot_of < own_count)
    down = kind == 1.0
    w_re = jnp.where(down, level * table(lambda k: coef_ref[0, k], modes, mode), 1.0) * near
    w_im = jnp.where(down, level * table(lambda k: coef_ref[1, k], modes, mode), 0.0) * near
    rate = jnp.where(down, level * table(lambda k: rate_ref[k], modes, mode), 0.0)
    wide_b = row_at_ref.shape[0]

    def mixing(wide, index, mask, signs):
        from_re, from_im = [], []
        for g in range(slots):
            own = flag((iota((wide, wide_q), 0) == index) & (slot_of == float(g)) & mask)
            for re, im in signs:
                from_re.append(own * re)
                from_im.append(own * im)
        return jnp.concatenate(from_re, axis=0), jnp.concatenate(from_im, axis=0)

    def packets(count, at, mask):
        return flag((iota((count, wide_q), 0) == at) & mask).astype(bf16)

    def place(value, at):
        hi, lo = split(value)
        return mm_nt(hi, at) + mm_nt(lo, at)

    rank_tile = jnp.floor((rank_c + 0.5) * (1.0 / per_tile))
    at_tile = rank_tile * float(tiers * 8) + holder * 8.0
    at_tile += (rank_c - rank_tile * float(per_tile)) * float(parts)
    from_re, from_im = mixing(wide_m, mode, valid, ((w_im, -w_re), (w_re, w_im)))

    def column_mix(value, q):
        return place(value, packets(tiles * tiers * 8, at_tile + float(q), valid))

    if rows < 128:
        mix_c = [column_mix(from_re, 0), column_mix(from_im, 0)]
    else:
        mix_c = [
            column_mix(from_re, h) + column_mix(from_im, parts // 2 + h) for h in range(parts // 2)
        ]
    from_re, from_im = mixing(wide_b, local_mode, in_block, ((w_im, w_re), (-w_re, w_im)))
    at_row = holder * float(rw) + rank_r
    mix_r = place(from_re, packets(tiers * rw, at_row, in_block)) + place(
        from_im, packets(tiers * rw, at_row + float(rp), in_block)
    )
    row_lane = lax.broadcasted_iota(jnp.int32, (1, rows), 1)
    row_at_ref[...] = jnp.zeros_like(row_at_ref)
    for k in range(block):
        row_at_ref[k : k + 1, :] = flag(row_lane == site_ref[sy * block + k] - row_start)

    def dots(pairs):
        if rows % 128 == 0:
            return mm(
                jnp.concatenate([a for a, _ in pairs], axis=1),
                jnp.concatenate([b for _, b in pairs], axis=0),
            )
        return sum(mm(a, b) for a, b in pairs)

    width = h_hi.shape[1]
    cuts = levels // width

    def commute(p, n):
        hi, lo = z_hi.at[p], z_lo.at[p]
        at = slice(n * width, (n + 1) * width)
        near_hi, near_lo = hi[:, at], lo[:, at]
        pairs = [(loc_hi, near_hi), (loc_lo, near_hi), (loc_hi, near_lo)]
        pairs += [(near_hi, h_hi[n]), (near_hi, h_lo[n]), (near_lo, h_hi[n])]
        for side, there in ((2 * n, (n + 1) * width), (2 * n - 1, n * width - 128)):
            if 0 <= side < 2 * (cuts - 1):
                there = slice(there, there + 128)
                pairs += [(hi[:, there], cross_hi[side]), (hi[:, there], cross_lo[side])]
                pairs += [(lo[:, there], cross_hi[side])]
        return dots(pairs)

    def ghost(p):
        hi, lo = split(jnp.concatenate([halo_in[s, p] for s in range(2)], axis=0))
        rest = jnp.zeros((128 - 6 * edge, levels), bf16)
        return mm(ghost_h, jnp.concatenate([hi, hi, lo, rest], axis=0))

    for g in range(slots):
        live = flag(own_count > float(g))
        damp = jnp.sum(jnp.where(slot_of == float(g), rate, 0.0), axis=1, keepdims=True) * live
        for c in range(2):
            p = g * 2 + c
            sign = live if c == 0 else -live
            for n in range(cuts):
                at = slice(n * width, (n + 1) * width)
                mid = st[p][:, at] + (0.5 * step_size) * sl[p][:, at]
                d_buf[p, :, at] = sign * commute(g * 2 + 1 - c, n) - damp * mid
                base_ref[p, :, at] = live * (st[p][:, at] + (step_size / 6.0) * sl[p][:, at])

    @pl.when(sy > 0)
    def _():
        halo(0).wait_recv()

    @pl.when(sy < systems - 1)
    def _():
        halo(1).wait_recv()

    for g in range(slots):
        live = flag(own_count > float(g))
        for c in range(2):
            extra = (live if c == 0 else -live) * ghost(g * 2 + 1 - c)
            d_buf[g * 2 + c, 0:edge, :] += extra[0:edge]
            d_buf[g * 2 + c, rows - edge : rows, :] += extra[edge : 2 * edge]

    calls(lambda n, turn, t: request(t, me).wait_send())
    calls(lambda n, turn, t: pack(n, turn, t, me).wait_send())

    @pl.when(sy < systems - 1)
    def _():
        halo(0).wait_send()

    @pl.when(sy > 0)
    def _():
        halo(1).wait_send()

    calls(lambda n, turn, t: pack(n, turn, t, t).wait_recv())
    got_c = jnp.concatenate(
        [recv_buf[:, levels + n * 128 : levels + (n + 1) * 128] for n in range(tiles)], axis=0
    )
    got_r = recv_buf[:, 0:levels]
    r_ref[...] = mm3(mix_r, got_r)
    if rows < 128:
        c_ref[...] = mm3(mix_c[0], got_c[:, :rows]) + mm3(mix_c[1], got_c[:, rows:])
    else:
        for h in range(parts // 2):
            c_ref[:, h * 128 : (h + 1) * 128] = mm3(mix_c[h], got_c)


def finish_kernel(
    cuts, spread_ref, row_at_ref, c_ref, r_ref, d_ref, base_ref, next_hbm, sum_hbm, next_buf, sum_buf, sem
):
    planes, rows, _ = d_ref.shape
    wide_m, wide_b = spread_ref.shape[0], row_at_ref.shape[0]
    ring, part = next_buf.shape[0], next_buf.shape[1]
    spread = spread_ref[...].astype(bf16)
    row_at = row_at_ref[...]

    def copies(n):
        at = pl.ds(n % cuts * part, part)
        slot = n % ring
        return (
            pltpu.make_async_copy(next_buf.at[slot], next_hbm.at[n // cuts, at], sem.at[0, slot]),
            pltpu.make_async_copy(sum_buf.at[slot], sum_hbm.at[n // cuts, at], sem.at[1, slot]),
        )

    for p in range(planes):
        col = c_ref[p * wide_m : (p + 1) * wide_m, :]
        col_hi = col.astype(bf16).astype(f32)
        left = jnp.concatenate([col_hi, col - col_hi, row_at, row_at], axis=0)
        left = jnp.transpose(left).astype(bf16)
        row_hi, row_lo = split(r_ref[p * wide_b : (p + 1) * wide_b, :])
        right = jnp.concatenate([spread, spread, row_hi, row_lo], axis=0)
        for q in range(cuts):
            n = p * cuts + q
            slot = n % ring
            if n >= ring:
                for copy in copies(n - ring):
                    copy.wait()
            at = slice(q * part, (q + 1) * part)
            slope_next = d_ref[p, at, :] + mm(left[at], right)
            next_buf[slot] = slope_next
            sum_buf[slot] = base_ref[p, at, :] + step_size / 3.0 * slope_next
            for copy in copies(n):
                copy.start()
    for n in range(planes * cuts - ring, planes * cuts):
        for copy in copies(n):
            copy.wait()


def order(layers, layer):
    table = [
        sorted(range(layers), key=lambda n: (n == at, -abs(n - at), n)) for at in range(layers)
    ]
    result = []
    for n in range(layers):
        value = table[0][n]
        for at in range(1, layers):
            value = jnp.where(layer == at, table[at][n], value)
        result.append(value)
    return result


def layer_size(mesh):
    tiers = mesh.shape["tier"]
    devices = mesh.devices[:, 0]
    if not hasattr(devices[0], "coords"):
        return tiers
    places = [tuple(device.coords) for device in devices]
    runs = [
        1 + sum(a[axis] != b[axis] for a, b in zip(places, places[1:]))
        for axis in range(len(places[0]))
    ]
    return tiers // min(count for count in runs + [tiers] if count > 1)


def shards(tiers, systems, group, state, slope, counts, links, mode_site, mode_coef, mode_rate, h_bands):
    slots, _, rows, levels = state.shape
    edge = h_bands.shape[0] - 1
    modes = mode_site.shape[0]
    block = modes // systems
    per_slot = links.shape[2]
    total = slots * per_slot
    cp = total // tiers
    rp = 2 * -(-(slots * block) // tiers)
    parts = 2 * rows // 128
    packet = up(cp * parts, 8)
    cj, rw = packet // parts, up(2 * rp, 8)
    wide_m, wide_b = up(modes, 16), up(block, 16)
    arrays = (links, counts, mode_site, mode_coef, mode_rate, h_bands, state, slope)
    vmem = pl.BlockSpec(memory_space=pltpu.VMEM)
    hbm = pl.BlockSpec(memory_space=pltpu.HBM)
    planes = slots * 2
    wide_rp = up(2 * slots * block, 128)
    dma = pltpu.SemaphoreType.DMA
    big = (planes, rows, levels)
    width = 256 if levels % 256 == 0 else levels
    deriv, base, col_mix, row_mix, spread, row_at = pl.pallas_call(
        functools.partial(
            exchange_kernel, (tiers, systems, group, slots, modes, block, edge, per_slot, rp, cj, rw)
        ),
        out_shape=(
            pltpu.VMEM(big, f32),
            pltpu.VMEM(big, f32),
            pltpu.VMEM((planes * wide_m, rows), f32),
            pltpu.VMEM((planes * wide_b, levels), f32),
            pltpu.VMEM((wide_m, levels), f32),
            pltpu.VMEM((wide_b, rows), f32),
        ),
        in_specs=[hbm] * 8,
        out_specs=(vmem,) * 6,
        scratch_shapes=[
            pltpu.VMEM(links.shape, jnp.int32),
            pltpu.SMEM(counts.shape, jnp.int32),
            pltpu.SMEM(mode_site.shape, jnp.int32),
            pltpu.SMEM(mode_coef.shape, f32),
            pltpu.SMEM(mode_rate.shape, f32),
            pltpu.VMEM(h_bands.shape, f32),
            (pltpu.VMEM((rows, levels), f32),) * planes,
            (pltpu.VMEM((rows, levels), f32),) * planes,
            pltpu.VMEM((planes, rows, levels), bf16),
            pltpu.VMEM((planes, rows, levels), bf16),
            pltpu.VMEM((levels // width, width, width), bf16),
            pltpu.VMEM((levels // width, width, width), bf16),
            pltpu.VMEM((tiers, 1, 128), f32),
            pltpu.VMEM((tiers, 1, 128), f32),
            pltpu.VMEM((2, planes, edge, levels), f32),
            pltpu.VMEM((2, planes, edge, levels), f32),
            pltpu.VMEM((2 * (levels // width), 128, width), bf16),
            pltpu.VMEM((2 * (levels // width), 128, width), bf16),
            pltpu.VMEM((parts, slots * wide_m, 128), bf16),
            pltpu.VMEM((parts, slots * wide_m, 128), bf16),
            pltpu.VMEM((wide_rp, levels), f32),
            pltpu.VMEM((tiers * rw, levels + packet * 16), f32),
            pltpu.VMEM((tiers * rw, levels + packet * 16), f32),
            dma((2, planes)),
            dma((tiers,)),
            dma((tiers,)),
            dma((2,)),
            dma((2,)),
            dma((tiers,)),
            dma((tiers,)),
            dma((6,)),
            pltpu.SemaphoreType.REGULAR((tiers // group,)),
            pltpu.SemaphoreType.REGULAR,
        ],
        compiler_params=pltpu.CompilerParams(
            collective_id=0, has_side_effects=True, vmem_limit_bytes=32 << 20
        ),
        name="exchange",
    )(*(pltpu.with_memory_space_constraint(x, pltpu.HBM) for x in arrays))
    cuts, ring = 1, 8
    outs = pl.pallas_call(
        functools.partial(finish_kernel, cuts),
        out_shape=(jax.ShapeDtypeStruct(big, f32),) * 2,
        in_specs=[vmem] * 6,
        out_specs=(hbm, hbm),
        scratch_shapes=[
            pltpu.VMEM((ring, rows // cuts, levels), f32),
            pltpu.VMEM((ring, rows // cuts, levels), f32),
            dma((2, ring)),
        ],
        compiler_params=pltpu.CompilerParams(vmem_limit_bytes=24 << 20),
        name="finish",
    )(spread, row_at, col_mix, row_mix, deriv, base)
    return tuple(out.reshape(state.shape) for out in outs)


def solution(mesh):
    in_specs = (
        P("tier", None, "sys", None),
        P("tier", None, "sys", None),
        P(),
        P(None, "tier", None),
        P(),
        P(),
        P(),
        P(),
    )
    out_specs = (P("tier", None, "sys", None), P("tier", None, "sys", None))
    body = functools.partial(shards, mesh.shape["tier"], mesh.shape["sys"], layer_size(mesh))
    return jax.shard_map(body, mesh=mesh, in_specs=in_specs, out_specs=out_specs, check_vma=False)
```

```python
import functools

import jax
import jax.numpy as jnp
from jax import lax
from jax.experimental import pallas as pl
from jax.experimental.pallas import tpu as pltpu
from jax.sharding import PartitionSpec as P

step_size = 0.05
MESH = pl.DeviceIdType.MESH
f32 = jnp.float32
bf16 = jnp.bfloat16


def up(value, unit):
    return (value + unit - 1) // unit * unit


def split(value):
    hi = value.astype(bf16)
    lo = (value - hi.astype(f32)).astype(bf16)
    return hi, lo


def mm(a, b):
    return lax.dot_general(a, b, (((1,), (0,)), ((), ())), preferred_element_type=f32)


def mm_nt(a, b):
    return lax.dot_general(a, b, (((1,), (1,)), ((), ())), preferred_element_type=f32)


def mm3(a, b):
    a_hi, a_lo = split(a)
    b_hi, b_lo = split(b)
    return mm(a_hi, b_hi) + (mm(a_hi, b_lo) + mm(a_lo, b_hi))


def exchange_kernel(
    dims,
    links_hbm,
    counts_hbm,
    site_hbm,
    coef_hbm,
    rate_hbm,
    bands_hbm,
    state_hbm,
    slope_hbm,
    d_buf,
    base_ref,
    c_ref,
    r_ref,
    spread_ref,
    row_at_ref,
    links_ref,
    counts_ref,
    site_ref,
    coef_ref,
    rate_ref,
    bands_ref,
    st,
    sl,
    z_hi,
    z_lo,
    h_hi,
    h_lo,
    req_ref,
    req_in,
    halo_out,
    halo_in,
    cross_hi,
    cross_lo,
    col_hi,
    col_lo,
    row_pack,
    send_buf,
    recv_buf,
    load_sem,
    req_send,
    req_recv,
    halo_send,
    halo_recv,
    pack_send,
    pack_recv,
    small_sem,
    here_sem,
    near_sem,
):
    tiers, systems, group, slots, modes, block, edge, per_slot, rp, cj, rw = dims
    rows, levels = st[0].shape
    me = lax.axis_index("tier")
    sy = lax.axis_index("sys")
    planes = slots * 2
    layers = tiers // group
    layer = me // group
    wide_m = spread_ref.shape[0]
    parts = 2 * rows // 128
    per_tile = 8 // parts
    tiles = cj // per_tile
    visits = order(layers, layer)
    place_in = me - layer * group
    first = layer * group

    def load(p):
        g, c = p // 2, p % 2
        return (
            pltpu.make_async_copy(state_hbm.at[g, c], st[p], load_sem.at[0, p]),
            pltpu.make_async_copy(slope_hbm.at[g, c], sl[p], load_sem.at[1, p]),
        )

    small = [
        pltpu.make_async_copy(src, dst, small_sem.at[n])
        for n, (src, dst) in enumerate(
            (
                (links_hbm, links_ref),
                (counts_hbm, counts_ref),
                (site_hbm, site_ref),
                (coef_hbm, coef_ref),
                (rate_hbm, rate_ref),
                (bands_hbm, bands_ref),
            )
        )
    ]
    for copy in small:
        copy.start()

    barrier = pltpu.get_barrier_semaphore()

    turns = [lax.rem(place_in + i, group) for i in range(group)]

    def greet(t):
        pl.semaphore_signal(barrier, inc=1, device_id=(t, sy), device_id_type=MESH)

    def mates(act):
        for i in range(1, group):
            act(first + turns[i])

    def layer_at(step, act):
        @pl.when((layer + step >= 0) & (layer + step < layers))
        def _():
            for i in range(group):
                act((layer + step) * group + turns[i])

    mates(greet)
    for step in range(1, layers):
        layer_at(step, greet)

    @pl.when(sy < systems - 1)
    def _():
        pl.semaphore_signal(barrier, inc=1, device_id=(me, sy + 1), device_id_type=MESH)

    def announce(t):
        pl.semaphore_signal(here_sem.at[layer], inc=1, device_id=(t, sy), device_id_type=MESH)

    pl.semaphore_wait(barrier, first + group - 1 + (sy > 0).astype(jnp.int32))
    for step in range(layers - 1, 0, -1):
        layer_at(-step, announce)

    @pl.when(sy > 0)
    def _():
        pl.semaphore_signal(near_sem, inc=1, device_id=(me, sy - 1), device_id_type=MESH)

    for p in range(planes):
        for copy in load(p):
            copy.start()

    total = slots * per_slot
    wide_q = up(total, 128)

    def iota(shape, axis):
        return lax.broadcasted_iota(jnp.int32, shape, axis).astype(f32)

    def flag(where):
        return jnp.where(where, 1.0, 0.0)

    for copy in small:
        copy.wait()
    flat = jnp.zeros((4, wide_q), f32)
    for g in range(slots):
        place = flag(
            iota((per_slot, wide_q), 1) == iota((per_slot, wide_q), 0) + float(g * per_slot)
        )
        flat += mm(links_ref[:, g, :].astype(f32).astype(bf16), place.astype(bf16))
    lane_q = iota((1, wide_q), 1)
    valid = lane_q < float(total)
    mode, kind, level = flat[1:2], flat[2:3], flat[3:4]
    holder = jnp.floor((flat[0:1] + 0.5) * (1.0 / slots))
    target = flat[0:1] - holder * float(slots)
    holder = jnp.where(valid, holder, -1.0)
    slot_of = jnp.where(valid, jnp.floor((lane_q + 0.5) * (1.0 / per_slot)), -1.0)
    first_mode = (sy * block).astype(f32)
    in_block = valid & (mode >= first_mode) & (mode < first_mode + float(block))
    local_mode = mode - first_mode
    has = flag(holder == iota((tiers, wide_q), 0))
    has_r = has * flag(in_block)
    before = flag(iota((wide_q, wide_q), 0) < iota((wide_q, wide_q), 1)).astype(bf16)
    rank_c = jnp.sum(has * mm(has.astype(bf16), before), axis=0, keepdims=True)
    rank_r = jnp.sum(has_r * mm(has_r.astype(bf16), before), axis=0, keepdims=True)
    lane_j = iota((128, wide_q), 0)

    def asked(codes, ranks):
        return mm_nt(codes.astype(bf16), flag(lane_j == ranks).astype(bf16))

    req = asked(has * (target * float(wide_m) + mode + 1.0), rank_c) - 1.0
    for c in range(2):
        code = (target + float(c * slots)) * float(block) + local_mode + 1.0
        req += asked(has_r * code, rank_r + float(8 + c * rp))
    for t in range(tiers):
        req_ref[t] = req[t : t + 1, :]
    req_in[me] = req_ref[me]

    def request(t, other):
        return pltpu.make_async_remote_copy(
            src_ref=req_ref.at[t],
            dst_ref=req_in.at[other],
            send_sem=req_send.at[t],
            recv_sem=req_recv.at[other],
            device_id=(t, sy),
            device_id_type=MESH,
        )

    def ask(t):
        request(t, me).start()

    for step in range(layers - 1, 0, -1):
        layer_at(-step, ask)
    mates(ask)

    def ask_above(step):
        @pl.when(layer + step < layers)
        def _():
            pl.semaphore_wait(here_sem.at[layer + step], group)

        layer_at(step, ask)

    for step in range(1, layers):
        ask_above(step)

    row_pack[...] = jnp.zeros_like(row_pack)
    col_hi[...] = jnp.zeros_like(col_hi)
    col_lo[...] = jnp.zeros_like(col_lo)
    site_lane = lax.broadcasted_iota(jnp.int32, (1, levels), 1)
    spread_ref[...] = jnp.zeros_like(spread_ref)
    for k in range(modes):
        spread_ref[k : k + 1, :] = flag(site_lane == site_ref[k])
    pick = spread_ref[...].astype(bf16)
    for g in range(slots):
        for c in range(2):
            p = g * 2 + c
            for copy in load(p):
                copy.wait()
            mid = st[p][...] + (0.5 * step_size) * sl[p][...]
            halo_out[0, p] = mid[rows - edge :, :]
            halo_out[1, p] = mid[:edge, :]
            hi, lo = split(mid)
            z_hi[p] = hi
            z_lo[p] = lo
            at = slice(g * wide_m, (g + 1) * wide_m)
            for dest, part in ((col_hi, hi), (col_lo, lo)):
                cols = mm_nt(pick, part).astype(bf16)
                for h in range(-(-rows // 128)):
                    q = c * rows // 128 + h
                    lane = c * rows % 128
                    dest[q, at, lane : lane + min(rows, 128)] = cols[:, h * 128 : h * 128 + 128]
            for k in range(block):
                at = jnp.clip(site_ref[sy * block + k] - sy * rows, 0, rows - 1)
                row = st[p][pl.ds(at, 1), :] + (0.5 * step_size) * sl[p][pl.ds(at, 1), :]
                dest = (c * slots + g) * block + k
                row_pack[dest : dest + 1, :] = row

    def halo(side):
        return pltpu.make_async_remote_copy(
            src_ref=halo_out.at[side],
            dst_ref=halo_in.at[side],
            send_sem=halo_send.at[side],
            recv_sem=halo_recv.at[side],
            device_id=(me, sy + 1 if side == 0 else sy - 1),
            device_id_type=MESH,
        )

    @pl.when(sy > 0)
    def _():
        halo(1).start()

    @pl.when(sy < systems - 1)
    def _():
        pl.semaphore_wait(near_sem, 1)
        halo(0).start()

    @pl.when(sy == 0)
    def _():
        halo_in[0] = jnp.zeros_like(halo_in[0])

    @pl.when(sy == systems - 1)
    def _():
        halo_in[1] = jnp.zeros_like(halo_in[1])

    def pack(n, turn, t, other):
        at = pl.multiple_of((n * group + turn) * rw, rw)
        return pltpu.make_async_remote_copy(
            src_ref=send_buf.at[pl.ds(at, rw), :],
            dst_ref=recv_buf.at[pl.ds(pl.multiple_of(other * rw, rw), rw), :],
            send_sem=pack_send.at[n * group + turn],
            recv_sem=pack_recv.at[other],
            device_id=(t, sy),
            device_id_type=MESH,
        )

    def calls(act):
        for n in range(layers):
            for i in range(1 if n == layers - 1 else 0, group):
                act(n, turns[i], visits[n] * group + turns[i])

    row_hi, row_lo = split(row_pack[...])
    per_c, per_r = tiles * group * 8, group * rw
    index = iota((per_c, 128), 0)
    tile = jnp.floor((index + 0.5) * (1.0 / (group * 8)))
    index -= tile * float(group * 8)
    owner = jnp.floor((index + 0.5) * (1.0 / 8))
    index -= owner * 8.0
    column = jnp.floor((index + 0.5) * (1.0 / parts))
    part_of = index - column * float(parts)
    wanted = tile * float(per_tile) + column
    index = iota((per_r, 128), 0)
    owner_r = jnp.floor((index + 0.5) * (1.0 / rw))
    wanted_r = index - owner_r * float(rw) + 8.0
    owner = jnp.concatenate([owner, owner_r], axis=0)
    spot = flag(jnp.concatenate([wanted, wanted_r], axis=0) == iota((per_c + per_r, 128), 1))
    expand = flag(owner[:, 0:1] == iota((per_c + per_r, group), 1)).astype(bf16)
    wide_k = parts * slots * wide_m
    wanted_at = iota((per_c, wide_k), 1) - part_of[:, 0:1] * float(slots * wide_m)
    in_part = (wanted_at >= 0.0) & (wanted_at < float(slots * wide_m))
    wanted_at = jnp.where(in_part, wanted_at, -2.0)
    wanted_row = iota((per_r, row_pack.shape[0]), 1)
    for n in range(layers):
        start = visits[n] * group
        for i in range(1 if n == layers - 1 else 0, group):
            request(start + turns[i], start + turns[i]).wait_recv()
        codes = mm(expand, req_in[pl.ds(start, group), 0, :].astype(bf16))
        code = jnp.sum(codes * spot, axis=1, keepdims=True)
        pick_c = flag(code[:per_c] == wanted_at).astype(bf16)
        pick_r = flag(code[per_c:] == wanted_row).astype(bf16)
        packed = mm(pick_c, col_hi[...].reshape(wide_k, 128)) + mm(
            pick_c, col_lo[...].reshape(wide_k, 128)
        )
        here = slice(n * group * rw, (n + 1) * group * rw)
        send_buf[here, 0:levels] = mm(pick_r, row_hi) + mm(pick_r, row_lo)
        for k in range(tiles):
            send_buf[here, levels + k * 128 : levels + (k + 1) * 128] = packed[
                k * group * 8 : (k + 1) * group * 8
            ]
        for i in range(1 if n == layers - 1 else 0, group):
            pack(n, turns[i], start + turns[i], me).start()
    own = pl.multiple_of(((layers - 1) * group + place_in) * rw, rw)
    recv_buf[pl.ds(pl.multiple_of(me * rw, rw), rw), :] = send_buf[pl.ds(own, rw), :]

    row_start = sy * rows
    blocks = levels // 128
    over = h_hi.shape[1] // 128
    diff = lax.broadcasted_iota(jnp.int32, (128, 128), 0) - lax.broadcasted_iota(
        jnp.int32, (128, 128), 1
    )
    bands = bands_ref[...]
    moved = [bands[o : o + 1, :] if o == 0 else pltpu.roll(bands, o, 1)[o : o + 1, :] for o in range(edge + 1)]

    def block_of(row, b):
        return row[:, b * 128 : (b + 1) * 128]

    def keep(hi_ref, lo_ref, n, row, lane, value):
        hi, lo = split(-value)
        high, wide = value.shape
        hi_ref[n, row : row + high, lane : lane + wide] = hi
        lo_ref[n, row : row + high, lane : lane + wide] = lo

    for ref in (h_hi, h_lo, cross_hi, cross_lo):
        ref[...] = jnp.zeros_like(ref)
    for b in range(blocks):
        value = jnp.where(diff == 0, block_of(bands[0:1, :], b), 0.0)
        for o in range(1, edge + 1):
            value = jnp.where(diff == o, block_of(bands[o : o + 1, :], b), value)
            value = jnp.where(diff == -o, block_of(moved[o], b), value)
        n, at = b // over, b % over * 128
        keep(h_hi, h_lo, n, at, at, value)
    corner = 2 * edge
    slant = diff[0:corner, :]
    for b in range(blocks - 1):
        above = jnp.zeros((corner, 128), f32)
        below = jnp.zeros((corner, 128), f32)
        for o in range(1, edge + 1):
            above = jnp.where(slant == corner - o, block_of(moved[o], b + 1), above)
            below = jnp.where(slant == o - 128, block_of(bands[o : o + 1, :], b), below)
        n, at = b // over, b % over * 128
        if b % over < over - 1:
            keep(h_hi, h_lo, n, at + 128 - corner, at + 128, above)
            keep(h_hi, h_lo, n, at + 128, at, below)
        else:
            keep(cross_hi, cross_lo, 2 * n, 0, at, below)
            keep(cross_hi, cross_lo, 2 * n + 1, 128 - corner, 0, above)

    def rolled(shift):
        return pltpu.roll(bands, lax.rem(shift + 2 * levels, levels), 1)

    if rows == h_hi.shape[1]:
        loc_hi, loc_lo = -h_hi[sy], -h_lo[sy]
    else:
        wide_r = up(rows, 128)
        gap = lax.broadcasted_iota(jnp.int32, (rows, wide_r), 0) - lax.broadcasted_iota(
            jnp.int32, (rows, wide_r), 1
        )
        near_bands = rolled(-row_start)
        loc = jnp.where(gap == 0, near_bands[0:1, :wide_r], 0.0)
        for o in range(1, edge + 1):
            loc = jnp.where(gap == o, near_bands[o : o + 1, :wide_r], loc)
            loc = jnp.where(gap == -o, pltpu.roll(near_bands, o, 1)[o : o + 1, :wide_r], loc)
        loc_hi, loc_lo = split(loc[:, :rows])
    sub = lax.broadcasted_iota(jnp.int32, (2 * edge, 128), 0)
    lan = lax.broadcasted_iota(jnp.int32, (2 * edge, 128), 1)
    low_bands = rolled(edge - row_start)
    high_bands = rolled(edge - row_start - rows)
    halo_h = jnp.zeros((2 * edge, 128), f32)
    for o in range(edge + 1):
        low = (sub < edge) & (lan < edge) & (edge + sub - lan == o)
        high = (sub >= edge) & (lan >= edge) & (lan < 2 * edge) & (edge + lan - sub == o)
        above = pltpu.roll(high_bands, o, 1) if o else high_bands
        halo_h = jnp.where(low, low_bands[o : o + 1, :128], halo_h)
        halo_h = jnp.where(high, above[o : o + 1, :128], halo_h)
    ghost_hi, ghost_lo = split(halo_h)
    ghost_h = jnp.where(lan < 2 * edge, ghost_hi.astype(f32), 0.0)
    ghost_h += pltpu.roll(jnp.where(lan < 2 * edge, ghost_lo.astype(f32), 0.0), 2 * edge, 1)
    ghost_h += pltpu.roll(jnp.where(lan < 2 * edge, ghost_hi.astype(f32), 0.0), 4 * edge, 1)
    ghost_h = ghost_h.astype(bf16)

    def table(ref, count, index):
        value = jnp.zeros((1, wide_q), f32)
        for k in range(count):
            value = jnp.where(index == float(k), ref(k), value)
        return value

    own_count = counts_ref[me].astype(f32)
    near = flag(target < table(lambda k: counts_ref[k].astype(f32), tiers, holder))
    near = near * flag(slot_of < own_count)
    down = kind == 1.0
    w_re = jnp.where(down, level * table(lambda k: coef_ref[0, k], modes, mode), 1.0) * near
    w_im = jnp.where(down, level * table(lambda k: coef_ref[1, k], modes, mode), 0.0) * near
    rate = jnp.where(down, level * table(lambda k: rate_ref[k], modes, mode), 0.0)
    wide_b = row_at_ref.shape[0]

    def mixing(wide, index, mask, signs):
        from_re, from_im = [], []
        for g in range(slots):
            own = flag((iota((wide, wide_q), 0) == index) & (slot_of == float(g)) & mask)
            for re, im in signs:
                from_re.append(own * re)
                from_im.append(own * im)
        return jnp.concatenate(from_re, axis=0), jnp.concatenate(from_im, axis=0)

    def packets(count, at, mask):
        return flag((iota((count, wide_q), 0) == at) & mask).astype(bf16)

    def place(value, at):
        hi, lo = split(value)
        return mm_nt(hi, at) + mm_nt(lo, at)

    rank_tile = jnp.floor((rank_c + 0.5) * (1.0 / per_tile))
    at_tile = rank_tile * float(tiers * 8) + holder * 8.0
    at_tile += (rank_c - rank_tile * float(per_tile)) * float(parts)
    from_re, from_im = mixing(wide_m, mode, valid, ((w_im, -w_re), (w_re, w_im)))

    def column_mix(value, q):
        return place(value, packets(tiles * tiers * 8, at_tile + float(q), valid))

    if rows < 128:
        mix_c = [column_mix(from_re, 0), column_mix(from_im, 0)]
    else:
        mix_c = [
            column_mix(from_re, h) + column_mix(from_im, parts // 2 + h) for h in range(parts // 2)
        ]
    from_re, from_im = mixing(wide_b, local_mode, in_block, ((w_im, w_re), (-w_re, w_im)))
    at_row = holder * float(rw) + rank_r
    mix_r = place(from_re, packets(tiers * rw, at_row, in_block)) + place(
        from_im, packets(tiers * rw, at_row + float(rp), in_block)
    )
    row_lane = lax.broadcasted_iota(jnp.int32, (1, rows), 1)
    row_at_ref[...] = jnp.zeros_like(row_at_ref)
    for k in range(block):
        row_at_ref[k : k + 1, :] = flag(row_lane == site_ref[sy * block + k] - row_start)

    def thrice(value):
        hi, lo = split(value)
        return jnp.concatenate([hi, hi, lo], axis=1)

    def stacked(value):
        hi, lo = split(value)
        return jnp.concatenate([hi, lo, hi], axis=0)

    mix_r = thrice(mix_r)
    mix_c = [thrice(value) for value in mix_c]

    def dots(pairs):
        if rows % 128 == 0:
            return mm(
                jnp.concatenate([a for a, _ in pairs], axis=1),
                jnp.concatenate([b for _, b in pairs], axis=0),
            )
        return sum(mm(a, b) for a, b in pairs)

    width = h_hi.shape[1]
    cuts = levels // width

    def commute(p, n):
        hi, lo = z_hi.at[p], z_lo.at[p]
        at = slice(n * width, (n + 1) * width)
        near_hi, near_lo = hi[:, at], lo[:, at]
        pairs = [(loc_hi, near_hi), (loc_lo, near_hi), (loc_hi, near_lo)]
        pairs += [(near_hi, h_hi[n]), (near_hi, h_lo[n]), (near_lo, h_hi[n])]
        for side, there in ((2 * n, (n + 1) * width), (2 * n - 1, n * width - 128)):
            if 0 <= side < 2 * (cuts - 1):
                there = slice(there, there + 128)
                pairs += [(hi[:, there], cross_hi[side]), (hi[:, there], cross_lo[side])]
                pairs += [(lo[:, there], cross_hi[side])]
        return dots(pairs)

    def ghost(p):
        hi, lo = split(jnp.concatenate([halo_in[s, p] for s in range(2)], axis=0))
        rest = jnp.zeros((128 - 6 * edge, levels), bf16)
        return mm(ghost_h, jnp.concatenate([hi, hi, lo, rest], axis=0))

    for g in range(slots):
        live = flag(own_count > float(g))
        damp = jnp.sum(jnp.where(slot_of == float(g), rate, 0.0), axis=1, keepdims=True) * live
        for c in range(2):
            p = g * 2 + c
            sign = live if c == 0 else -live
            for n in range(cuts):
                at = slice(n * width, (n + 1) * width)
                mid = st[p][:, at] + (0.5 * step_size) * sl[p][:, at]
                d_buf[p, :, at] = sign * commute(g * 2 + 1 - c, n) - damp * mid
                base_ref[p, :, at] = live * (st[p][:, at] + (step_size / 6.0) * sl[p][:, at])

    @pl.when(sy > 0)
    def _():
        halo(0).wait_recv()

    @pl.when(sy < systems - 1)
    def _():
        halo(1).wait_recv()

    for g in range(slots):
        live = flag(own_count > float(g))
        for c in range(2):
            extra = (live if c == 0 else -live) * ghost(g * 2 + 1 - c)
            d_buf[g * 2 + c, 0:edge, :] += extra[0:edge]
            d_buf[g * 2 + c, rows - edge : rows, :] += extra[edge : 2 * edge]

    calls(lambda n, turn, t: request(t, me).wait_send())
    calls(lambda n, turn, t: pack(n, turn, t, me).wait_send())

    @pl.when(sy < systems - 1)
    def _():
        halo(0).wait_send()

    @pl.when(sy > 0)
    def _():
        halo(1).wait_send()

    calls(lambda n, turn, t: pack(n, turn, t, t).wait_recv())
    got_r = stacked(recv_buf[:, 0:levels])
    got_c = jnp.concatenate(
        [recv_buf[:, levels + n * 128 : levels + (n + 1) * 128] for n in range(tiles)], axis=0
    )
    got_c = stacked(got_c)
    if rows < 128:
        c_ref[...] = mm(mix_c[0], got_c[:, :rows]) + mm(mix_c[1], got_c[:, rows:])
    else:
        both = mm(jnp.concatenate(mix_c, axis=0), got_c)
        high = c_ref.shape[0]
        for h in range(parts // 2):
            c_ref[:, h * 128 : (h + 1) * 128] = both[h * high : (h + 1) * high]
    r_ref[...] = mm(mix_r, got_r)


def finish_kernel(
    cuts, spread_ref, row_at_ref, c_ref, r_ref, d_ref, base_ref, next_hbm, sum_hbm, next_buf, sum_buf, sem
):
    planes, rows, _ = d_ref.shape
    wide_m, wide_b = spread_ref.shape[0], row_at_ref.shape[0]
    ring, part = next_buf.shape[0], next_buf.shape[1]
    spread = spread_ref[...].astype(bf16)
    row_at = row_at_ref[...]

    def copies(n):
        at = pl.ds(n % cuts * part, part)
        slot = n % ring
        return (
            pltpu.make_async_copy(next_buf.at[slot], next_hbm.at[n // cuts, at], sem.at[0, slot]),
            pltpu.make_async_copy(sum_buf.at[slot], sum_hbm.at[n // cuts, at], sem.at[1, slot]),
        )

    for p in range(planes):
        col = c_ref[p * wide_m : (p + 1) * wide_m, :]
        col_hi = col.astype(bf16).astype(f32)
        left = jnp.concatenate([col_hi, col - col_hi, row_at, row_at], axis=0)
        left = jnp.transpose(left).astype(bf16)
        row_hi, row_lo = split(r_ref[p * wide_b : (p + 1) * wide_b, :])
        right = jnp.concatenate([spread, spread, row_hi, row_lo], axis=0)
        for q in range(cuts):
            n = p * cuts + q
            slot = n % ring
            if n >= ring:
                for copy in copies(n - ring):
                    copy.wait()
            at = slice(q * part, (q + 1) * part)
            slope_next = d_ref[p, at, :] + mm(left[at], right)
            next_buf[slot] = slope_next
            sum_buf[slot] = base_ref[p, at, :] + step_size / 3.0 * slope_next
            for copy in copies(n):
                copy.start()
    for n in range(planes * cuts - ring, planes * cuts):
        for copy in copies(n):
            copy.wait()


def order(layers, layer):
    table = [
        sorted(range(layers), key=lambda n: (n == at, -abs(n - at), n)) for at in range(layers)
    ]
    result = []
    for n in range(layers):
        value = table[0][n]
        for at in range(1, layers):
            value = jnp.where(layer == at, table[at][n], value)
        result.append(value)
    return result


def layer_size(mesh):
    tiers = mesh.shape["tier"]
    devices = mesh.devices[:, 0]
    if not hasattr(devices[0], "coords"):
        return tiers
    places = [tuple(device.coords) for device in devices]
    runs = [
        1 + sum(a[axis] != b[axis] for a, b in zip(places, places[1:]))
        for axis in range(len(places[0]))
    ]
    return tiers // min(count for count in runs + [tiers] if count > 1)


def shards(tiers, systems, group, state, slope, counts, links, mode_site, mode_coef, mode_rate, h_bands):
    slots, _, rows, levels = state.shape
    edge = h_bands.shape[0] - 1
    modes = mode_site.shape[0]
    block = modes // systems
    per_slot = links.shape[2]
    total = slots * per_slot
    cp = total // tiers
    rp = 2 * -(-(slots * block) // tiers)
    parts = 2 * rows // 128
    packet = up(cp * parts, 8)
    cj, rw = packet // parts, up(2 * rp, 8)
    wide_m, wide_b = up(modes, 16), up(block, 16)
    arrays = (links, counts, mode_site, mode_coef, mode_rate, h_bands, state, slope)
    vmem = pl.BlockSpec(memory_space=pltpu.VMEM)
    hbm = pl.BlockSpec(memory_space=pltpu.HBM)
    planes = slots * 2
    wide_rp = up(2 * slots * block, 128)
    dma = pltpu.SemaphoreType.DMA
    big = (planes, rows, levels)
    width = 256 if levels % 256 == 0 else levels
    deriv, base, col_mix, row_mix, spread, row_at = pl.pallas_call(
        functools.partial(
            exchange_kernel, (tiers, systems, group, slots, modes, block, edge, per_slot, rp, cj, rw)
        ),
        out_shape=(
            pltpu.VMEM(big, f32),
            pltpu.VMEM(big, f32),
            pltpu.VMEM((planes * wide_m, rows), f32),
            pltpu.VMEM((planes * wide_b, levels), f32),
            pltpu.VMEM((wide_m, levels), f32),
            pltpu.VMEM((wide_b, rows), f32),
        ),
        in_specs=[hbm] * 8,
        out_specs=(vmem,) * 6,
        scratch_shapes=[
            pltpu.VMEM(links.shape, jnp.int32),
            pltpu.SMEM(counts.shape, jnp.int32),
            pltpu.SMEM(mode_site.shape, jnp.int32),
            pltpu.SMEM(mode_coef.shape, f32),
            pltpu.SMEM(mode_rate.shape, f32),
            pltpu.VMEM(h_bands.shape, f32),
            (pltpu.VMEM((rows, levels), f32),) * planes,
            (pltpu.VMEM((rows, levels), f32),) * planes,
            pltpu.VMEM((planes, rows, levels), bf16),
            pltpu.VMEM((planes, rows, levels), bf16),
            pltpu.VMEM((levels // width, width, width), bf16),
            pltpu.VMEM((levels // width, width, width), bf16),
            pltpu.VMEM((tiers, 1, 128), f32),
            pltpu.VMEM((tiers, 1, 128), f32),
            pltpu.VMEM((2, planes, edge, levels), f32),
            pltpu.VMEM((2, planes, edge, levels), f32),
            pltpu.VMEM((2 * (levels // width), 128, width), bf16),
            pltpu.VMEM((2 * (levels // width), 128, width), bf16),
            pltpu.VMEM((parts, slots * wide_m, 128), bf16),
            pltpu.VMEM((parts, slots * wide_m, 128), bf16),
            pltpu.VMEM((wide_rp, levels), f32),
            pltpu.VMEM((tiers * rw, levels + packet * 16), f32),
            pltpu.VMEM((tiers * rw, levels + packet * 16), f32),
            dma((2, planes)),
            dma((tiers,)),
            dma((tiers,)),
            dma((2,)),
            dma((2,)),
            dma((tiers,)),
            dma((tiers,)),
            dma((6,)),
            pltpu.SemaphoreType.REGULAR((tiers // group,)),
            pltpu.SemaphoreType.REGULAR,
        ],
        compiler_params=pltpu.CompilerParams(
            collective_id=0, has_side_effects=True, vmem_limit_bytes=32 << 20
        ),
        name="exchange",
    )(*(pltpu.with_memory_space_constraint(x, pltpu.HBM) for x in arrays))
    cuts, ring = 1, 8
    outs = pl.pallas_call(
        functools.partial(finish_kernel, cuts),
        out_shape=(jax.ShapeDtypeStruct(big, f32),) * 2,
        in_specs=[vmem] * 6,
        out_specs=(hbm, hbm),
        scratch_shapes=[
            pltpu.VMEM((ring, rows // cuts, levels), f32),
            pltpu.VMEM((ring, rows // cuts, levels), f32),
            dma((2, ring)),
        ],
        compiler_params=pltpu.CompilerParams(vmem_limit_bytes=24 << 20),
        name="finish",
    )(spread, row_at, col_mix, row_mix, deriv, base)
    return tuple(out.reshape(state.shape) for out in outs)


def solution(mesh):
    in_specs = (
        P("tier", None, "sys", None),
        P("tier", None, "sys", None),
        P(),
        P(None, "tier", None),
        P(),
        P(),
        P(),
        P(),
    )
    out_specs = (P("tier", None, "sys", None), P("tier", None, "sys", None))
    body = functools.partial(shards, mesh.shape["tier"], mesh.shape["sys"], layer_size(mesh))
    return jax.shard_map(body, mesh=mesh, in_specs=in_specs, out_specs=out_specs, check_vma=False)
```

```python
import functools

import jax
import jax.numpy as jnp
from jax import lax
from jax.experimental import pallas as pl
from jax.experimental.pallas import tpu as pltpu
from jax.sharding import PartitionSpec as P

step_size = 0.05
MESH = pl.DeviceIdType.MESH
f32 = jnp.float32
bf16 = jnp.bfloat16


def up(value, unit):
    return (value + unit - 1) // unit * unit


def split(value):
    hi = value.astype(bf16)
    lo = (value - hi.astype(f32)).astype(bf16)
    return hi, lo


def mm(a, b):
    return lax.dot_general(a, b, (((1,), (0,)), ((), ())), preferred_element_type=f32)


def mm_nt(a, b):
    return lax.dot_general(a, b, (((1,), (1,)), ((), ())), preferred_element_type=f32)


def mm3(a, b):
    a_hi, a_lo = split(a)
    b_hi, b_lo = split(b)
    return mm(a_hi, b_hi) + (mm(a_hi, b_lo) + mm(a_lo, b_hi))


def exchange_kernel(
    dims,
    links_hbm,
    counts_hbm,
    site_hbm,
    coef_hbm,
    rate_hbm,
    bands_hbm,
    state_hbm,
    slope_hbm,
    d_buf,
    base_ref,
    c_ref,
    r_ref,
    spread_ref,
    row_at_ref,
    links_ref,
    counts_ref,
    site_ref,
    coef_ref,
    rate_ref,
    bands_ref,
    st,
    sl,
    z_hi,
    z_lo,
    h_hi,
    h_lo,
    req_ref,
    req_in,
    halo_out,
    halo_in,
    cross_hi,
    cross_lo,
    col_hi,
    col_lo,
    row_pack,
    send_buf,
    recv_buf,
    load_sem,
    req_send,
    req_recv,
    halo_send,
    halo_recv,
    pack_send,
    pack_recv,
    small_sem,
    here_sem,
    near_sem,
):
    tiers, systems, group, slots, modes, block, edge, per_slot, rp, cj, rw = dims
    rows, levels = st[0].shape
    me = lax.axis_index("tier")
    sy = lax.axis_index("sys")
    planes = slots * 2
    layers = tiers // group
    layer = me // group
    wide_m = spread_ref.shape[0]
    parts = 2 * rows // 128
    per_tile = 8 // parts
    tiles = cj // per_tile
    visits = order(layers, layer)
    place_in = me - layer * group
    first = layer * group

    def load(p):
        g, c = p // 2, p % 2
        return (
            pltpu.make_async_copy(state_hbm.at[g, c], st[p], load_sem.at[0, p]),
            pltpu.make_async_copy(slope_hbm.at[g, c], sl[p], load_sem.at[1, p]),
        )

    small = [
        pltpu.make_async_copy(src, dst, small_sem.at[n])
        for n, (src, dst) in enumerate(
            (
                (links_hbm, links_ref),
                (counts_hbm, counts_ref),
                (site_hbm, site_ref),
                (coef_hbm, coef_ref),
                (rate_hbm, rate_ref),
                (bands_hbm, bands_ref),
            )
        )
    ]
    for copy in small:
        copy.start()

    barrier = pltpu.get_barrier_semaphore()

    turns = [lax.rem(place_in + i, group) for i in range(group)]

    def greet(t):
        pl.semaphore_signal(barrier, inc=1, device_id=(t, sy), device_id_type=MESH)

    def mates(act):
        for i in range(1, group):
            act(first + turns[i])

    def layer_at(step, act):
        @pl.when((layer + step >= 0) & (layer + step < layers))
        def _():
            for i in range(group):
                act((layer + step) * group + turns[i])

    mates(greet)
    for step in range(1, layers):
        layer_at(step, greet)

    @pl.when(sy < systems - 1)
    def _():
        pl.semaphore_signal(barrier, inc=1, device_id=(me, sy + 1), device_id_type=MESH)

    def announce(t):
        pl.semaphore_signal(here_sem.at[layer], inc=1, device_id=(t, sy), device_id_type=MESH)

    pl.semaphore_wait(barrier, first + group - 1 + (sy > 0).astype(jnp.int32))
    for step in range(layers - 1, 0, -1):
        layer_at(-step, announce)

    @pl.when(sy > 0)
    def _():
        pl.semaphore_signal(near_sem, inc=1, device_id=(me, sy - 1), device_id_type=MESH)

    for p in range(planes):
        for copy in load(p):
            copy.start()

    total = slots * per_slot
    wide_q = up(total, 128)

    def iota(shape, axis):
        return lax.broadcasted_iota(jnp.int32, shape, axis).astype(f32)

    def flag(where):
        return jnp.where(where, 1.0, 0.0)

    for copy in small:
        copy.wait()
    flat = jnp.zeros((4, wide_q), f32)
    for g in range(slots):
        place = flag(
            iota((per_slot, wide_q), 1) == iota((per_slot, wide_q), 0) + float(g * per_slot)
        )
        flat += mm(links_ref[:, g, :].astype(f32).astype(bf16), place.astype(bf16))
    lane_q = iota((1, wide_q), 1)
    valid = lane_q < float(total)
    mode, kind, level = flat[1:2], flat[2:3], flat[3:4]
    holder = jnp.floor((flat[0:1] + 0.5) * (1.0 / slots))
    target = flat[0:1] - holder * float(slots)
    holder = jnp.where(valid, holder, -1.0)
    slot_of = jnp.where(valid, jnp.floor((lane_q + 0.5) * (1.0 / per_slot)), -1.0)
    first_mode = (sy * block).astype(f32)
    in_block = valid & (mode >= first_mode) & (mode < first_mode + float(block))
    local_mode = mode - first_mode
    has = flag(holder == iota((tiers, wide_q), 0))
    has_r = has * flag(in_block)
    before = flag(iota((wide_q, wide_q), 0) < iota((wide_q, wide_q), 1)).astype(bf16)
    rank_c = jnp.sum(has * mm(has.astype(bf16), before), axis=0, keepdims=True)
    rank_r = jnp.sum(has_r * mm(has_r.astype(bf16), before), axis=0, keepdims=True)
    lane_j = iota((128, wide_q), 0)

    def asked(codes, ranks):
        return mm_nt(codes.astype(bf16), flag(lane_j == ranks).astype(bf16))

    req = asked(has * (target * float(wide_m) + mode + 1.0), rank_c) - 1.0
    for c in range(2):
        code = (target + float(c * slots)) * float(block) + local_mode + 1.0
        req += asked(has_r * code, rank_r + float(8 + c * rp))
    for t in range(tiers):
        req_ref[t] = req[t : t + 1, :]
    req_in[me] = req_ref[me]

    def request(t, other):
        return pltpu.make_async_remote_copy(
            src_ref=req_ref.at[t],
            dst_ref=req_in.at[other],
            send_sem=req_send.at[t],
            recv_sem=req_recv.at[other],
            device_id=(t, sy),
            device_id_type=MESH,
        )

    def ask(t):
        request(t, me).start()

    for step in range(layers - 1, 0, -1):
        layer_at(-step, ask)
    mates(ask)

    def ask_above(step):
        @pl.when(layer + step < layers)
        def _():
            pl.semaphore_wait(here_sem.at[layer + step], group)

        layer_at(step, ask)

    for step in range(1, layers):
        ask_above(step)

    row_pack[...] = jnp.zeros_like(row_pack)
    col_hi[...] = jnp.zeros_like(col_hi)
    col_lo[...] = jnp.zeros_like(col_lo)
    site_lane = lax.broadcasted_iota(jnp.int32, (1, levels), 1)
    spread_ref[...] = jnp.zeros_like(spread_ref)
    for k in range(modes):
        spread_ref[k : k + 1, :] = flag(site_lane == site_ref[k])
    pick = spread_ref[...].astype(bf16)
    for g in range(slots):
        for c in range(2):
            p = g * 2 + c
            for copy in load(p):
                copy.wait()
            mid = st[p][...] + (0.5 * step_size) * sl[p][...]
            halo_out[0, p] = mid[rows - edge :, :]
            halo_out[1, p] = mid[:edge, :]
            hi, lo = split(mid)
            z_hi[p] = hi
            z_lo[p] = lo
            at = slice(g * wide_m, (g + 1) * wide_m)
            for dest, part in ((col_hi, hi), (col_lo, lo)):
                cols = mm_nt(pick, part).astype(bf16)
                for h in range(-(-rows // 128)):
                    q = c * rows // 128 + h
                    lane = c * rows % 128
                    dest[q, at, lane : lane + min(rows, 128)] = cols[:, h * 128 : h * 128 + 128]
            for k in range(block):
                at = jnp.clip(site_ref[sy * block + k] - sy * rows, 0, rows - 1)
                row = st[p][pl.ds(at, 1), :] + (0.5 * step_size) * sl[p][pl.ds(at, 1), :]
                dest = (c * slots + g) * block + k
                row_pack[dest : dest + 1, :] = row

    def halo(side):
        return pltpu.make_async_remote_copy(
            src_ref=halo_out.at[side],
            dst_ref=halo_in.at[side],
            send_sem=halo_send.at[side],
            recv_sem=halo_recv.at[side],
            device_id=(me, sy + 1 if side == 0 else sy - 1),
            device_id_type=MESH,
        )

    @pl.when(sy > 0)
    def _():
        halo(1).start()

    @pl.when(sy < systems - 1)
    def _():
        pl.semaphore_wait(near_sem, 1)
        halo(0).start()

    @pl.when(sy == 0)
    def _():
        halo_in[0] = jnp.zeros_like(halo_in[0])

    @pl.when(sy == systems - 1)
    def _():
        halo_in[1] = jnp.zeros_like(halo_in[1])

    def pack(n, turn, t, other):
        at = pl.multiple_of((n * group + turn) * rw, rw)
        return pltpu.make_async_remote_copy(
            src_ref=send_buf.at[pl.ds(at, rw), :],
            dst_ref=recv_buf.at[pl.ds(pl.multiple_of(other * rw, rw), rw), :],
            send_sem=pack_send.at[n * group + turn],
            recv_sem=pack_recv.at[other],
            device_id=(t, sy),
            device_id_type=MESH,
        )

    def calls(act):
        for n in range(layers):
            for i in range(1 if n == layers - 1 else 0, group):
                act(n, turns[i], visits[n] * group + turns[i])

    row_hi, row_lo = split(row_pack[...])
    per_c, per_r = tiles * group * 8, group * rw
    index = iota((per_c, 128), 0)
    tile = jnp.floor((index + 0.5) * (1.0 / (group * 8)))
    index -= tile * float(group * 8)
    owner = jnp.floor((index + 0.5) * (1.0 / 8))
    index -= owner * 8.0
    column = jnp.floor((index + 0.5) * (1.0 / parts))
    part_of = index - column * float(parts)
    wanted = tile * float(per_tile) + column
    index = iota((per_r, 128), 0)
    owner_r = jnp.floor((index + 0.5) * (1.0 / rw))
    wanted_r = index - owner_r * float(rw) + 8.0
    owner = jnp.concatenate([owner, owner_r], axis=0)
    spot = flag(jnp.concatenate([wanted, wanted_r], axis=0) == iota((per_c + per_r, 128), 1))
    expand = flag(owner[:, 0:1] == iota((per_c + per_r, group), 1)).astype(bf16)
    wide_k = parts * slots * wide_m
    wanted_at = iota((per_c, wide_k), 1) - part_of[:, 0:1] * float(slots * wide_m)
    in_part = (wanted_at >= 0.0) & (wanted_at < float(slots * wide_m))
    wanted_at = jnp.where(in_part, wanted_at, -2.0)
    wanted_row = iota((per_r, row_pack.shape[0]), 1)
    for n in range(layers):
        start = visits[n] * group
        for i in range(1 if n == layers - 1 else 0, group):
            request(start + turns[i], start + turns[i]).wait_recv()
        codes = mm(expand, req_in[pl.ds(start, group), 0, :].astype(bf16))
        code = jnp.sum(codes * spot, axis=1, keepdims=True)
        pick_c = flag(code[:per_c] == wanted_at).astype(bf16)
        pick_r = flag(code[per_c:] == wanted_row).astype(bf16)
        packed = mm(pick_c, col_hi[...].reshape(wide_k, 128)) + mm(
            pick_c, col_lo[...].reshape(wide_k, 128)
        )
        here = slice(n * group * rw, (n + 1) * group * rw)
        send_buf[here, 0:levels] = mm(pick_r, row_hi) + mm(pick_r, row_lo)
        for k in range(tiles):
            send_buf[here, levels + k * 128 : levels + (k + 1) * 128] = packed[
                k * group * 8 : (k + 1) * group * 8
            ]
        for i in range(1 if n == layers - 1 else 0, group):
            pack(n, turns[i], start + turns[i], me).start()
    own = pl.multiple_of(((layers - 1) * group + place_in) * rw, rw)
    recv_buf[pl.ds(pl.multiple_of(me * rw, rw), rw), :] = send_buf[pl.ds(own, rw), :]

    row_start = sy * rows
    blocks = levels // 128
    over = h_hi.shape[1] // 128
    diff = lax.broadcasted_iota(jnp.int32, (128, 128), 0) - lax.broadcasted_iota(
        jnp.int32, (128, 128), 1
    )
    bands = bands_ref[...]
    moved = [bands[o : o + 1, :] if o == 0 else pltpu.roll(bands, o, 1)[o : o + 1, :] for o in range(edge + 1)]

    def block_of(row, b):
        return row[:, b * 128 : (b + 1) * 128]

    def keep(hi_ref, lo_ref, n, row, lane, value):
        hi, lo = split(-value)
        high, wide = value.shape
        hi_ref[n, row : row + high, lane : lane + wide] = hi
        lo_ref[n, row : row + high, lane : lane + wide] = lo

    for ref in (h_hi, h_lo, cross_hi, cross_lo):
        ref[...] = jnp.zeros_like(ref)
    for b in range(blocks):
        value = jnp.where(diff == 0, block_of(bands[0:1, :], b), 0.0)
        for o in range(1, edge + 1):
            value = jnp.where(diff == o, block_of(bands[o : o + 1, :], b), value)
            value = jnp.where(diff == -o, block_of(moved[o], b), value)
        n, at = b // over, b % over * 128
        keep(h_hi, h_lo, n, at, at, value)
    corner = 2 * edge
    slant = diff[0:corner, :]
    for b in range(blocks - 1):
        above = jnp.zeros((corner, 128), f32)
        below = jnp.zeros((corner, 128), f32)
        for o in range(1, edge + 1):
            above = jnp.where(slant == corner - o, block_of(moved[o], b + 1), above)
            below = jnp.where(slant == o - 128, block_of(bands[o : o + 1, :], b), below)
        n, at = b // over, b % over * 128
        if b % over < over - 1:
            keep(h_hi, h_lo, n, at + 128 - corner, at + 128, above)
            keep(h_hi, h_lo, n, at + 128, at, below)
        else:
            keep(cross_hi, cross_lo, 2 * n, 0, at, below)
            keep(cross_hi, cross_lo, 2 * n + 1, 128 - corner, 0, above)

    def rolled(shift):
        return pltpu.roll(bands, lax.rem(shift + 2 * levels, levels), 1)

    if rows == h_hi.shape[1]:
        loc_hi, loc_lo = -h_hi[sy], -h_lo[sy]
    else:
        wide_r = up(rows, 128)
        gap = lax.broadcasted_iota(jnp.int32, (rows, wide_r), 0) - lax.broadcasted_iota(
            jnp.int32, (rows, wide_r), 1
        )
        near_bands = rolled(-row_start)
        loc = jnp.where(gap == 0, near_bands[0:1, :wide_r], 0.0)
        for o in range(1, edge + 1):
            loc = jnp.where(gap == o, near_bands[o : o + 1, :wide_r], loc)
            loc = jnp.where(gap == -o, pltpu.roll(near_bands, o, 1)[o : o + 1, :wide_r], loc)
        loc_hi, loc_lo = split(loc[:, :rows])
    sub = lax.broadcasted_iota(jnp.int32, (2 * edge, 128), 0)
    lan = lax.broadcasted_iota(jnp.int32, (2 * edge, 128), 1)
    low_bands = rolled(edge - row_start)
    high_bands = rolled(edge - row_start - rows)
    halo_h = jnp.zeros((2 * edge, 128), f32)
    for o in range(edge + 1):
        low = (sub < edge) & (lan < edge) & (edge + sub - lan == o)
        high = (sub >= edge) & (lan >= edge) & (lan < 2 * edge) & (edge + lan - sub == o)
        above = pltpu.roll(high_bands, o, 1) if o else high_bands
        halo_h = jnp.where(low, low_bands[o : o + 1, :128], halo_h)
        halo_h = jnp.where(high, above[o : o + 1, :128], halo_h)
    ghost_hi, ghost_lo = split(halo_h)
    ghost_h = jnp.where(lan < 2 * edge, ghost_hi.astype(f32), 0.0)
    ghost_h += pltpu.roll(jnp.where(lan < 2 * edge, ghost_lo.astype(f32), 0.0), 2 * edge, 1)
    ghost_h += pltpu.roll(jnp.where(lan < 2 * edge, ghost_hi.astype(f32), 0.0), 4 * edge, 1)
    ghost_h = ghost_h.astype(bf16)

    def table(ref, count, index):
        value = jnp.zeros((1, wide_q), f32)
        for k in range(count):
            value = jnp.where(index == float(k), ref(k), value)
        return value

    own_count = counts_ref[me].astype(f32)
    near = flag(target < table(lambda k: counts_ref[k].astype(f32), tiers, holder))
    near = near * flag(slot_of < own_count)
    down = kind == 1.0
    w_re = jnp.where(down, level * table(lambda k: coef_ref[0, k], modes, mode), 1.0) * near
    w_im = jnp.where(down, level * table(lambda k: coef_ref[1, k], modes, mode), 0.0) * near
    rate = jnp.where(down, level * table(lambda k: rate_ref[k], modes, mode), 0.0)
    wide_b = row_at_ref.shape[0]

    def mixing(wide, index, mask, signs):
        from_re, from_im = [], []
        for g in range(slots):
            own = flag((iota((wide, wide_q), 0) == index) & (slot_of == float(g)) & mask)
            for re, im in signs:
                from_re.append(own * re)
                from_im.append(own * im)
        return jnp.concatenate(from_re, axis=0), jnp.concatenate(from_im, axis=0)

    def packets(count, at, mask):
        return flag((iota((count, wide_q), 0) == at) & mask).astype(bf16)

    def place(value, at):
        hi, lo = split(value)
        return mm_nt(hi, at) + mm_nt(lo, at)

    rank_tile = jnp.floor((rank_c + 0.5) * (1.0 / per_tile))
    at_tile = rank_tile * float(tiers * 8) + holder * 8.0
    at_tile += (rank_c - rank_tile * float(per_tile)) * float(parts)
    from_re, from_im = mixing(wide_m, mode, valid, ((w_im, -w_re), (w_re, w_im)))

    def column_mix(value, q):
        return place(value, packets(tiles * tiers * 8, at_tile + float(q), valid))

    if rows < 128:
        mix_c = [column_mix(from_re, 0), column_mix(from_im, 0)]
    else:
        mix_c = [
            column_mix(from_re, h) + column_mix(from_im, parts // 2 + h) for h in range(parts // 2)
        ]
    from_re, from_im = mixing(wide_b, local_mode, in_block, ((w_im, w_re), (-w_re, w_im)))
    at_row = holder * float(rw) + rank_r
    mix_r = place(from_re, packets(tiers * rw, at_row, in_block)) + place(
        from_im, packets(tiers * rw, at_row + float(rp), in_block)
    )
    row_lane = lax.broadcasted_iota(jnp.int32, (1, rows), 1)
    row_at_ref[...] = jnp.zeros_like(row_at_ref)
    for k in range(block):
        row_at_ref[k : k + 1, :] = flag(row_lane == site_ref[sy * block + k] - row_start)

    def thrice(value):
        hi, lo = split(value)
        return jnp.concatenate([hi, hi, lo], axis=1)

    def stacked(value):
        hi, lo = split(value)
        return jnp.concatenate([hi, lo, hi], axis=0)

    mix_r = thrice(mix_r)
    mix_c = [thrice(value) for value in mix_c]

    def dots(pairs):
        if rows % 128 == 0:
            return mm(
                jnp.concatenate([a for a, _ in pairs], axis=1),
                jnp.concatenate([b for _, b in pairs], axis=0),
            )
        return sum(mm(a, b) for a, b in pairs)

    width = h_hi.shape[1]
    cuts = levels // width

    def commute(p, n):
        hi, lo = z_hi.at[p], z_lo.at[p]
        at = slice(n * width, (n + 1) * width)
        near_hi, near_lo = hi[:, at], lo[:, at]
        pairs = [(loc_hi, near_hi), (loc_lo, near_hi), (loc_hi, near_lo)]
        pairs += [(near_hi, h_hi[n]), (near_hi, h_lo[n]), (near_lo, h_hi[n])]
        for side, there in ((2 * n, (n + 1) * width), (2 * n - 1, n * width - 128)):
            if 0 <= side < 2 * (cuts - 1):
                there = slice(there, there + 128)
                pairs += [(hi[:, there], cross_hi[side]), (hi[:, there], cross_lo[side])]
                pairs += [(lo[:, there], cross_hi[side])]
        return dots(pairs)

    def ghost(p):
        hi, lo = split(jnp.concatenate([halo_in[s, p] for s in range(2)], axis=0))
        rest = jnp.zeros((128 - 6 * edge, levels), bf16)
        return mm(ghost_h, jnp.concatenate([hi, hi, lo, rest], axis=0))

    for g in range(slots):
        live = flag(own_count > float(g))
        damp = jnp.sum(jnp.where(slot_of == float(g), rate, 0.0), axis=1, keepdims=True) * live
        for c in range(2):
            p = g * 2 + c
            sign = live if c == 0 else -live
            for n in range(cuts):
                at = slice(n * width, (n + 1) * width)
                mid = st[p][:, at] + (0.5 * step_size) * sl[p][:, at]
                d_buf[p, :, at] = sign * commute(g * 2 + 1 - c, n) - damp * mid
                base_ref[p, :, at] = live * (st[p][:, at] + (step_size / 6.0) * sl[p][:, at])

    @pl.when(sy > 0)
    def _():
        halo(0).wait_recv()

    @pl.when(sy < systems - 1)
    def _():
        halo(1).wait_recv()

    for g in range(slots):
        live = flag(own_count > float(g))
        for c in range(2):
            extra = (live if c == 0 else -live) * ghost(g * 2 + 1 - c)
            d_buf[g * 2 + c, 0:edge, :] += extra[0:edge]
            d_buf[g * 2 + c, rows - edge : rows, :] += extra[edge : 2 * edge]

    calls(lambda n, turn, t: request(t, me).wait_send())
    calls(lambda n, turn, t: pack(n, turn, t, me).wait_send())

    @pl.when(sy < systems - 1)
    def _():
        halo(0).wait_send()

    @pl.when(sy > 0)
    def _():
        halo(1).wait_send()

    calls(lambda n, turn, t: pack(n, turn, t, t).wait_recv())
    got_r = stacked(recv_buf[:, 0:levels])
    got_c = jnp.concatenate(
        [recv_buf[:, levels + n * 128 : levels + (n + 1) * 128] for n in range(tiles)], axis=0
    )
    got_c = stacked(got_c)
    if rows < 128:
        c_ref[...] = mm(mix_c[0], got_c[:, :rows]) + mm(mix_c[1], got_c[:, rows:])
    else:
        both = mm(jnp.concatenate(mix_c, axis=0), got_c)
        high = c_ref.shape[0]
        for h in range(parts // 2):
            c_ref[:, h * 128 : (h + 1) * 128] = both[h * high : (h + 1) * high]
    r_ref[...] = mm(mix_r, got_r)


def finish_kernel(
    cuts, spread_ref, row_at_ref, c_ref, r_ref, d_ref, base_ref, next_hbm, sum_hbm, next_buf, sum_buf, sem
):
    planes, rows, _ = d_ref.shape
    wide_m, wide_b = spread_ref.shape[0], row_at_ref.shape[0]
    ring, part = next_buf.shape[0], next_buf.shape[1]
    spread = spread_ref[...].astype(bf16)
    row_at = row_at_ref[...]

    def copies(n):
        at = pl.ds(n % cuts * part, part)
        slot = n % ring
        return (
            pltpu.make_async_copy(next_buf.at[slot], next_hbm.at[n // cuts, at], sem.at[0, slot]),
            pltpu.make_async_copy(sum_buf.at[slot], sum_hbm.at[n // cuts, at], sem.at[1, slot]),
        )

    for p in range(planes):
        col = c_ref[p * wide_m : (p + 1) * wide_m, :]
        col_hi = col.astype(bf16).astype(f32)
        left = jnp.concatenate([col_hi, col - col_hi, row_at, row_at], axis=0)
        left = jnp.transpose(left).astype(bf16)
        row_hi, row_lo = split(r_ref[p * wide_b : (p + 1) * wide_b, :])
        right = jnp.concatenate([spread, spread, row_hi, row_lo], axis=0)
        for q in range(cuts):
            n = p * cuts + q
            slot = n % ring
            if n >= ring:
                for copy in copies(n - ring):
                    copy.wait()
            at = slice(q * part, (q + 1) * part)
            slope_next = d_ref[p, at, :] + mm(left[at], right)
            to_next, to_sum = copies(n)
            next_buf[slot] = slope_next
            to_next.start()
            sum_buf[slot] = base_ref[p, at, :] + step_size / 3.0 * slope_next
            to_sum.start()
    for n in range(planes * cuts - ring, planes * cuts):
        for copy in copies(n):
            copy.wait()


def order(layers, layer):
    table = [
        sorted(range(layers), key=lambda n: (n == at, -abs(n - at), n)) for at in range(layers)
    ]
    result = []
    for n in range(layers):
        value = table[0][n]
        for at in range(1, layers):
            value = jnp.where(layer == at, table[at][n], value)
        result.append(value)
    return result


def layer_size(mesh):
    tiers = mesh.shape["tier"]
    devices = mesh.devices[:, 0]
    if not hasattr(devices[0], "coords"):
        return tiers
    places = [tuple(device.coords) for device in devices]
    runs = [
        1 + sum(a[axis] != b[axis] for a, b in zip(places, places[1:]))
        for axis in range(len(places[0]))
    ]
    return tiers // min(count for count in runs + [tiers] if count > 1)


def shards(tiers, systems, group, state, slope, counts, links, mode_site, mode_coef, mode_rate, h_bands):
    slots, _, rows, levels = state.shape
    edge = h_bands.shape[0] - 1
    modes = mode_site.shape[0]
    block = modes // systems
    per_slot = links.shape[2]
    total = slots * per_slot
    cp = total // tiers
    rp = 2 * -(-(slots * block) // tiers)
    parts = 2 * rows // 128
    packet = up(cp * parts, 8)
    cj, rw = packet // parts, up(2 * rp, 8)
    wide_m, wide_b = up(modes, 16), up(block, 16)
    arrays = (links, counts, mode_site, mode_coef, mode_rate, h_bands, state, slope)
    vmem = pl.BlockSpec(memory_space=pltpu.VMEM)
    hbm = pl.BlockSpec(memory_space=pltpu.HBM)
    planes = slots * 2
    wide_rp = up(2 * slots * block, 128)
    dma = pltpu.SemaphoreType.DMA
    big = (planes, rows, levels)
    width = 256 if levels % 256 == 0 else levels
    deriv, base, col_mix, row_mix, spread, row_at = pl.pallas_call(
        functools.partial(
            exchange_kernel, (tiers, systems, group, slots, modes, block, edge, per_slot, rp, cj, rw)
        ),
        out_shape=(
            pltpu.VMEM(big, f32),
            pltpu.VMEM(big, f32),
            pltpu.VMEM((planes * wide_m, rows), f32),
            pltpu.VMEM((planes * wide_b, levels), f32),
            pltpu.VMEM((wide_m, levels), f32),
            pltpu.VMEM((wide_b, rows), f32),
        ),
        in_specs=[hbm] * 8,
        out_specs=(vmem,) * 6,
        scratch_shapes=[
            pltpu.VMEM(links.shape, jnp.int32),
            pltpu.SMEM(counts.shape, jnp.int32),
            pltpu.SMEM(mode_site.shape, jnp.int32),
            pltpu.SMEM(mode_coef.shape, f32),
            pltpu.SMEM(mode_rate.shape, f32),
            pltpu.VMEM(h_bands.shape, f32),
            (pltpu.VMEM((rows, levels), f32),) * planes,
            (pltpu.VMEM((rows, levels), f32),) * planes,
            pltpu.VMEM((planes, rows, levels), bf16),
            pltpu.VMEM((planes, rows, levels), bf16),
            pltpu.VMEM((levels // width, width, width), bf16),
            pltpu.VMEM((levels // width, width, width), bf16),
            pltpu.VMEM((tiers, 1, 128), f32),
            pltpu.VMEM((tiers, 1, 128), f32),
            pltpu.VMEM((2, planes, edge, levels), f32),
            pltpu.VMEM((2, planes, edge, levels), f32),
            pltpu.VMEM((2 * (levels // width), 128, width), bf16),
            pltpu.VMEM((2 * (levels // width), 128, width), bf16),
            pltpu.VMEM((parts, slots * wide_m, 128), bf16),
            pltpu.VMEM((parts, slots * wide_m, 128), bf16),
            pltpu.VMEM((wide_rp, levels), f32),
            pltpu.VMEM((tiers * rw, levels + packet * 16), f32),
            pltpu.VMEM((tiers * rw, levels + packet * 16), f32),
            dma((2, planes)),
            dma((tiers,)),
            dma((tiers,)),
            dma((2,)),
            dma((2,)),
            dma((tiers,)),
            dma((tiers,)),
            dma((6,)),
            pltpu.SemaphoreType.REGULAR((tiers // group,)),
            pltpu.SemaphoreType.REGULAR,
        ],
        compiler_params=pltpu.CompilerParams(
            collective_id=0, has_side_effects=True, vmem_limit_bytes=32 << 20
        ),
        name="exchange",
    )(*(pltpu.with_memory_space_constraint(x, pltpu.HBM) for x in arrays))
    cuts, ring = 1, 8
    outs = pl.pallas_call(
        functools.partial(finish_kernel, cuts),
        out_shape=(jax.ShapeDtypeStruct(big, f32),) * 2,
        in_specs=[vmem] * 6,
        out_specs=(hbm, hbm),
        scratch_shapes=[
            pltpu.VMEM((ring, rows // cuts, levels), f32),
            pltpu.VMEM((ring, rows // cuts, levels), f32),
            dma((2, ring)),
        ],
        compiler_params=pltpu.CompilerParams(vmem_limit_bytes=24 << 20),
        name="finish",
    )(spread, row_at, col_mix, row_mix, deriv, base)
    return tuple(out.reshape(state.shape) for out in outs)


def solution(mesh):
    in_specs = (
        P("tier", None, "sys", None),
        P("tier", None, "sys", None),
        P(),
        P(None, "tier", None),
        P(),
        P(),
        P(),
        P(),
    )
    out_specs = (P("tier", None, "sys", None), P("tier", None, "sys", None))
    body = functools.partial(shards, mesh.shape["tier"], mesh.shape["sys"], layer_size(mesh))
    return jax.shard_map(body, mesh=mesh, in_specs=in_specs, out_specs=out_specs, check_vma=False)
```
